256 devices in a mesh: dp: 2 (over core), row: 32 (over z, x), col: 4 (over y).
Axes of the slice: x: 4, y: 4, z: 8, core: 2. Of those that a mesh axis runs over, the one named last changes fastest.
Arguments:
- inputs: bfloat16 [1024, 6144], P(('dp', 'row'), 'col'), may hold values from -6 to 6
- up_weight: bfloat16 [6144, 24576], P('col', ('dp', 'row')), may hold values from -0.078125 to 0.078125
- down_weight: bfloat16 [24576, 6144], P(('dp', 'row'), 'col'), may hold values from -0.0390625 to 0.0390625
- cotangent: bfloat16 [1024, 6144], P(('dp', 'row'), 'col'), may hold values from -3 to 3
Outputs:
- input_grad: bfloat16 [1024, 6144], P(('dp', 'row'), 'col')
- up_grad: bfloat16 [6144, 24576], P('col', ('dp', 'row'))
- down_grad: bfloat16 [24576, 6144], P(('dp', 'row'), 'col')
The draws below stay inside these ranges and needn't reach their ends.
All inputs are finite; a program needn't handle non-finite values.
Results may differ from the reference program's by a relative error of at most 0.0049.
Values may be sent and summed in bfloat16 or wider, within the bound.
A program may use at most 128 MiB of HBM per device.

```python
import math
import jax
import jax.numpy as jnp
from jax import lax

D = 6144
FF = 24576
TOKENS = 1024
N_DP = 2


def level_of(key, dims, split, low, top_value):
    def one(axis_at, shards_of):
        steps = jax.random.uniform(jax.random.fold_in(jax.random.fold_in(key, 6), axis_at), (shards_of,), jnp.float32, low / len(split), top_value / len(split))
        return jnp.repeat(jnp.exp(steps), dims[axis_at] // shards_of).reshape((-1,) + (1,) * (len(dims) - axis_at - 1))

    factor_of = one(*split[0])
    for cut in split[1:]:
        factor_of = factor_of * one(*cut)
    return factor_of


def normal_values(own_key, shape, scale, limit, split=(), kind=jnp.bfloat16):
    entries = jax.random.normal(own_key, shape, jnp.float32) * scale
    if len(split) > 0:
        entries = level_of(own_key, shape, split, -0.22, 0.18) * entries
    return jnp.clip(entries, min=-limit, max=limit).astype(kind)


def setup_inputs(seed: int = 0) -> dict:
    splits = jax.random.split(jax.random.key(seed), 5)
    return {
        "inputs": normal_values(splits[0], (TOKENS, D), 1.0, 6.0, ((0, 64), (1, 4))),
        "up_weight": normal_values(splits[1], (D, FF), D ** -0.5, 0.078125, ((0, 4), (1, 64))),
        "down_weight": normal_values(splits[2], (FF, D), FF ** -0.5, 0.0390625, ((0, 64), (1, 4))),
        "cotangent": normal_values(splits[3], (TOKENS, D), 0.5, 3.0, ((0, 64), (1, 4))),
    }


gelu_const = math.sqrt(2.0 / math.pi)

def gelu_tanh(value):
    inner = gelu_const * (value + 0.044715 * value * value * value)
    return 0.5 * value * (1.0 + jnp.tanh(inner))

def gelu_slope(value):
    tangent = jnp.tanh(gelu_const * (value + 0.044715 * value * value * value))
    return 0.5 * (1.0 + tangent) + 0.5 * value * (1.0 - tangent * tangent) * gelu_const * (1.0 + 3.0 * 0.044715 * value * value)

def reference(inputs, up_weight, down_weight, cotangent):
    hidden = jnp.dot(inputs, up_weight, preferred_element_type=jnp.float32)
    active = gelu_tanh(hidden).astype(jnp.bfloat16)
    delta_act = lax.dot_general(cotangent, down_weight, (((1,), (1,)), ((), ())), preferred_element_type=jnp.float32)
    delta = (delta_act * gelu_slope(hidden)).astype(jnp.bfloat16)
    input_grad = lax.dot_general(delta, up_weight, (((1,), (1,)), ((), ())), preferred_element_type=jnp.float32).astype(jnp.bfloat16)
    up_total = lax.dot_general(inputs, delta, (((0,), (0,)), ((), ())), preferred_element_type=jnp.float32)
    down_total = lax.dot_general(active, cotangent, (((0,), (0,)), ((), ())), preferred_element_type=jnp.float32)
    up_grad = (up_total / N_DP).astype(jnp.bfloat16)
    down_grad = (down_total / N_DP).astype(jnp.bfloat16)
    return (input_grad, up_grad, down_grad)
```

```python
import functools
import math

import jax
import jax.numpy as jnp
from jax import lax
from jax.experimental import pallas as pl
from jax.experimental.pallas import tpu as pltpu
from jax.sharding import Mesh
from jax.sharding import PartitionSpec as P

NZ, NX, NY = 8, 4, 4
DP_ROW = ("dp", "z", "x")
MESH = pl.DeviceIdType.MESH

CHUNKS = ((1, 7), (4, 0), (3, 5), (2, 6))

gelu_const = math.sqrt(2.0 / math.pi)
bf16, f32 = jnp.bfloat16, jnp.float32


def gelu_and_slope(value):
    tangent = jnp.tanh(gelu_const * (value + 0.044715 * value * value * value))
    half = 0.5 * (1.0 + tangent)
    slope = half + 0.5 * value * (1.0 - tangent * tangent) * gelu_const * (
        1.0 + 3.0 * 0.044715 * value * value
    )
    return value * half, slope


def contract(left, right, dims):
    return lax.dot_general(left, right, ((dims[:1], dims[1:]), ((), ())), preferred_element_type=f32)


class at:
    def __init__(self, ref):
        self.ref, self.index = ref, ()

    def __getitem__(self, index):
        self.index = index
        return self

    def __call__(self):
        return self.ref.at[self.index]


class Names:
    def __init__(self):
        self.known = {}

    def __call__(self, name):
        return self.known.setdefault(name, len(self.known))


def kernel(
    x_hbm, g_hbm, wu_hbm, wd_hbm, dx_out, up_out, down_out,
    XG, WU, WD, PART, PART16, R1, S2, R2, AD, AT, Q, PS, PR,
    ZS, ZR, XS, XR, XSF, XRF, LS, LR, LSF, LRF, local_sem, send_sem, recv_sem,
):
    width, units = WU.shape
    half = width // 2
    core, z, x, y = (lax.axis_index(a) for a in ("dp", "z", "x", "y"))
    partner = {"dp": 1 - core}
    left_z, right_z = {"z": (z + NZ - 1) % NZ}, {"z": (z + 1) % NZ}
    left_x, right_x = {"x": (x + NX - 1) % NX}, {"x": (x + 1) % NX}
    ya = y + 1 - 2 * (y % 2)
    yb = 3 - y
    yab = 3 - ya
    near_a, near_b = {"y": ya}, {"y": yb}

    sends, names = Names(), Names()
    started = {None: [], 0: [], 1: []}
    side = [None]

    def send(src, dst, device, name):
        number = sends((side[0], len(started[side[0]])))
        pltpu.make_async_remote_copy(
            src_ref=src(),
            dst_ref=dst(),
            send_sem=send_sem.at[number],
            recv_sem=recv_sem.at[names(name)],
            device_id=device,
            device_id_type=MESH,
        ).start()
        started[side[0]].append((src, number))

    def recv(dst, name):
        pltpu.make_async_remote_copy(
            src_ref=dst(),
            dst_ref=dst(),
            send_sem=send_sem.at[0],
            recv_sem=recv_sem.at[names(name)],
            device_id=partner,
            device_id_type=MESH,
        ).wait_recv()

    def sent(src, number):
        pltpu.make_async_remote_copy(
            src_ref=src(),
            dst_ref=src(),
            send_sem=send_sem.at[number],
            recv_sem=recv_sem.at[0],
            device_id=partner,
            device_id_type=MESH,
        ).wait_send()

    def on_core(number, body):
        @pl.when(core == number)
        def _():
            side[0] = number
            body()
            side[0] = None

    local = []
    for k, (src, dst) in enumerate(
        ((x_hbm, XG.at[0, 0, 0, 0]), (g_hbm, XG.at[0, 0, 0, 1]), (wu_hbm, WU), (wd_hbm, WD))
    ):
        local.append(pltpu.make_async_copy(src, dst, local_sem.at[k]))
        local[-1].start()

    barrier = pltpu.get_barrier_semaphore()
    near = (partner, left_z, right_z, left_x, right_x, near_a, near_b)
    for device in near:
        pl.semaphore_signal(barrier, inc=1, device_id=device, device_id_type=MESH)
    pl.semaphore_wait(barrier, len(near))
    local[0].wait()
    local[1].wait()

    def block(pz, px, a=None, k=0):
        return at(XG)[k, pz, px] if a is None else at(XG)[k, pz, px, a]

    def hand(pz_from, pz_to, px_from, px_to, device, a=None):
        send(block(pz_from, px_from, a), block(pz_to, px_to, a), device, ("xg", pz_to, px_to, a))

    def get(pz, px, a=None):
        recv(block(pz, px, a), ("xg", pz, px, a))

    def spread_z(px):
        hand(0, NZ - 1, px, px, right_z)
        hand(0, 1, px, px, left_z)

    def spread_x(pz):
        hand(pz, pz, 0, NX - 1, right_x)
        hand(pz, pz, 0, 1, left_x)

    def relay_x(pz):
        get(pz, 3)
        hand(pz, pz, 3, 2, right_x, 0)
        get(pz, 1)
        hand(pz, pz, 1, 2, left_x, 1)

    def end_x(pz):
        get(pz, 2, 0)
        get(pz, 2, 1)

    def relay_z(d, px):
        last = d == NZ // 2 - 1
        get(NZ - d, px)
        hand(NZ - d, NZ - d - 1, px, px, right_z, 0 if last else None)
        get(d, px)
        hand(d, d + 1, px, px, left_z, 1 if last else None)

    def end_z(px):
        get(NZ // 2, px, 0)
        get(NZ // 2, px, 1)

    def to_partner(*groups):
        for pz in groups:
            send(at(XG)[0, pz], at(XG)[1, pz], partner, ("pair", pz))

    def gather(step):
        def x_then_z():
            if step == 0:
                spread_x(0)
                spread_z(0)
                get(0, 3)
                hand(0, 0, 3, 2, right_x, 0)
                spread_z(3)
                get(0, 1)
                hand(0, 0, 1, 2, left_x, 1)
                spread_z(1)
                end_x(0)
                spread_z(2)
                to_partner(0)
            elif step < 4:
                for px in (0, 3, 1, 2):
                    relay_z(step, px)
                to_partner(NZ - step, step)
            else:
                for px in (0, 3, 1, 2):
                    end_z(px)
                to_partner(4)

        def z_then_x():
            if step == 0:
                spread_z(0)
                spread_x(0)
                relay_z(1, 0)
                spread_x(7)
                spread_x(1)
                relay_x(0)
                relay_z(2, 0)
                spread_x(6)
                spread_x(2)
                relay_x(7)
                relay_x(1)
                end_x(0)
                to_partner(0)
            elif step == 1:
                relay_z(3, 0)
                spread_x(5)
                spread_x(3)
                relay_x(6)
                relay_x(2)
                end_x(7)
                end_x(1)
                to_partner(7, 1)
            elif step == 2:
                end_z(0)
                spread_x(4)
                relay_x(5)
                relay_x(3)
                end_x(6)
                end_x(2)
                to_partner(6, 2)
            elif step == 3:
                relay_x(4)
                end_x(5)
                end_x(3)
                to_partner(5, 3)
            else:
                end_x(4)
                to_partner(4)

        on_core(0, x_then_z)
        on_core(1, z_then_x)

    def tokens(j, a, columns=slice(None)):
        return [
            XG[k, pz, :, a, :, columns].reshape(NX * 16, -1) for pz in CHUNKS[j] for k in range(2)
        ]

    def products(j):
        for pz in CHUNKS[j]:
            recv(at(XG)[1, pz], ("pair", pz))
        for a, (weights, dims) in enumerate(((WU, (1, 0)), (WD, (1, 1)))):
            part = contract(jnp.concatenate(tokens(j, a), axis=0), weights[...], dims)
            part = part.reshape(4, NX * 16, units)
            PART[j, a] = part
            PART16[j, a] = part.astype(bf16)
        for a, device, first in ((0, near_a, ya), (1, near_b, yb)):
            for k, owner in ((1, yab), (0, first)):
                send(at(PART16)[j, a, owner], at(R1)[j, a, k], device, ("r1", j, a, k))

    def second_sum(j):
        for a, device, owner in ((0, near_b, yb), (1, near_a, ya)):
            recv(at(R1)[j, a, 1], ("r1", j, a, 1))
            S2[j, a] = (PART[j, a, owner] + R1[j, a, 1].astype(f32)).astype(bf16)
            send(at(S2)[j, a], at(R2)[j, a], device, ("r2", j, a))

    def activate(j):
        sums = []
        for a in range(2):
            recv(at(R1)[j, a, 0], ("r1", j, a, 0))
            recv(at(R2)[j, a], ("r2", j, a))
            sums.append(PART[j, a, y] + R1[j, a, 0].astype(f32) + R2[j, a].astype(f32))
        active, slope = gelu_and_slope(sums[0])
        AD[j, 0, y] = active.astype(bf16)
        AD[j, 1, y] = (sums[1] * slope).astype(bf16)
        for a in range(2):
            send(at(AD)[j, a, y], at(AD)[j, a, y], near_b, ("ad", j, a, "b"))
            send(at(AD)[j, a, y], at(AD)[j, a, y], near_a, ("ad", j, a, "a"))

    def relay_y(j):
        recv(at(AD)[j, 0, yb], ("ad", j, 0, "b"))
        send(at(AD)[j, 0, yb], at(AD)[j, 0, yb], near_a, ("ad", j, 0, "ab"))
        recv(at(AD)[j, 1, ya], ("ad", j, 1, "a"))
        send(at(AD)[j, 1, ya], at(AD)[j, 1, ya], near_b, ("ad", j, 1, "ab"))

    def inward(j):
        recv(at(AD)[j, 0, ya], ("ad", j, 0, "a"))
        recv(at(AD)[j, 0, yab], ("ad", j, 0, "ab"))
        recv(at(AD)[j, 1, yb], ("ad", j, 1, "b"))
        recv(at(AD)[j, 1, yab], ("ad", j, 1, "ab"))
        delta = AD[j, 1].reshape(4 * NX * 16, units)
        back = contract(delta, WU[...], (1, 1)).reshape(4, NX, 16, width)
        for n, pz in enumerate(CHUNKS[j]):
            PS[pz] = back[2 * n + 1]
            send(at(PS)[pz], at(PR)[pz], partner, ("back", pz))
            Q[pz] = back[2 * n]

    def turn(j):
        rows = slice(j * 4 * NX * 16, (j + 1) * 4 * NX * 16)
        for a in range(2):
            AT[a, :, rows] = AD[j, a].reshape(4 * NX * 16, units).T

    def both(pz):
        recv(at(PR)[pz], ("back", pz))
        return Q[pz] + PR[pz]

    def add_at(value, low, part):
        wide = part.shape[-1]
        pieces = [value[..., low : low + wide] + part.astype(f32)]
        if low > 0:
            pieces.insert(0, value[..., :low])
        if low + wide < value.shape[-1]:
            pieces.append(value[..., low + wide :])
        return jnp.concatenate(pieces, axis=-1) if len(pieces) > 1 else pieces[0]

    lows = (0, half)

    def ring_z(hop):
        for s, device in enumerate((right_z, left_z)):
            pz = 4 - hop if s == 0 else (4 + hop)
            if hop == 0:
                continue
            value = both(pz)
            if hop == 1:
                recv(at(ZR)[s, 0, :, :, :half], ("z", s, 0))
                value = add_at(value, lows[s], ZR[s, 0, :, :, :half])
            else:
                recv(at(ZR)[s, hop - 1], ("z", s, hop - 1))
                value = value + ZR[s, hop - 1].astype(f32)
            ZS[s, hop] = value.astype(bf16)
            send(at(ZS)[s, hop], at(ZR)[s, hop], device, ("z", s, hop))

    def ring_z_first():
        value = both(4)
        for s, device in enumerate((right_z, left_z)):
            ZS[s, 0, :, :, :half] = value[..., lows[s] : lows[s] + half].astype(bf16)
            send(at(ZS)[s, 0, :, :, :half], at(ZR)[s, 0, :, :, :half], device, ("z", s, 0))

    def ring_z_last():
        value = both(0)
        for s in range(2):
            recv(at(ZR)[s, 3], ("z", s, 3))
            value = value + ZR[s, 3].astype(f32)
        Q[0] = value

    def line_x_first():
        for s, device in enumerate((right_x, left_x)):
            LS[s, 0, :, :half] = Q[0, 2, :, lows[s] : lows[s] + half].astype(bf16)
            send(at(LS)[s, 0, :, :half], at(LR)[s, 0, :, :half], device, ("line", s, 0))

    def line_x_second():
        for s, device in enumerate((right_x, left_x)):
            recv(at(LR)[s, 0, :, :half], ("line", s, 0))
            LSF[s] = add_at(Q[0, 1 + 2 * s], lows[s], LR[s, 0, :, :half])
            send(at(LSF)[s], at(LRF)[s], device, ("last", s))

    def last():
        value = Q[0, 0]
        for s in range(2):
            recv(at(LRF)[s], ("last", s))
            value = value + LRF[s]
        dx_out[...] = value.astype(bf16)

    def rows_x_first(pz):
        recv(at(PR)[pz], ("back", pz))
        value = Q[pz, 2] + PR[pz, 2]
        for s, device in enumerate((right_x, left_x)):
            XS[s, pz] = value[:, lows[s] : lows[s] + half].astype(bf16)
            send(at(XS)[s, pz], at(XR)[s, pz], device, ("x", s, pz))

    def rows_x_second(pz):
        for s, device in enumerate((right_x, left_x)):
            recv(at(XR)[s, pz], ("x", s, pz))
            value = Q[pz, 1 + 2 * s] + PR[pz, 1 + 2 * s]
            XSF[s, pz] = add_at(value, lows[s], XR[s, pz]).astype(bf16)
            send(at(XSF)[s, pz], at(XRF)[s, pz], device, ("xf", s, pz))

    def rows_x_last(pz):
        value = Q[pz, 0] + PR[pz, 0]
        for s in range(2):
            recv(at(XRF)[s, pz], ("xf", s, pz))
            value = value + XRF[s, pz].astype(f32)
        return value

    def line_z(hop):
        for s, device in enumerate((right_z, left_z)):
            value = rows_x_last(4 - hop if s == 0 else 4 + hop)
            if hop == 1:
                recv(at(LR)[s, 0, :, :half], ("line", s, 0))
                value = add_at(value, lows[s], LR[s, 0, :, :half])
            else:
                recv(at(LR)[s, hop - 1], ("line", s, hop - 1))
                value = value + LR[s, hop - 1].astype(f32)
            if hop < 3:
                LS[s, hop] = value.astype(bf16)
                send(at(LS)[s, hop], at(LR)[s, hop], device, ("line", s, hop))
            else:
                LSF[s] = value
                send(at(LSF)[s], at(LRF)[s], device, ("last", s))

    def line_z_first():
        value = rows_x_last(4)
        for s, device in enumerate((right_z, left_z)):
            LS[s, 0, :, :half] = value[:, lows[s] : lows[s] + half].astype(bf16)
            send(at(LS)[s, 0, :, :half], at(LR)[s, 0, :, :half], device, ("line", s, 0))

    def line_z_last():
        Q[0, 0] = rows_x_last(0)

    piece = min(256, width)

    def weight_piece(n, a):
        columns = slice(n * piece, (n + 1) * piece)
        every = jnp.concatenate([t for j in range(4) for t in tokens(j, a, columns)], axis=0)
        grad = contract(AT[1 - a], every, (1, 0)) * 0.5
        if a == 0:
            up_out[columns, :] = grad.T.astype(bf16)
        else:
            down_out[:, columns] = grad.astype(bf16)

    pieces = [(n, a) for a in (1, 0) for n in range(width // piece)]

    def weights_some(count):
        for _ in range(count):
            if pieces:
                weight_piece(*pieces.pop(0))

    gather(0)
    gather(1)
    local[2].wait()
    local[3].wait()
    products(0)
    gather(2)
    second_sum(0)
    gather(3)
    activate(0)
    gather(4)
    products(1)
    relay_y(0)
    second_sum(1)
    products(2)
    inward(0)
    on_core(1, lambda: [rows_x_first(pz) for pz in CHUNKS[0]])
    activate(1)
    second_sum(2)
    on_core(1, lambda: [rows_x_second(pz) for pz in CHUNKS[0]])
    products(3)
    relay_y(1)
    activate(2)
    second_sum(3)
    turn(0)
    inward(1)
    on_core(0, ring_z_first)
    on_core(1, lambda: [rows_x_first(pz) for pz in CHUNKS[1]])
    relay_y(2)
    activate(3)
    on_core(1, lambda: [rows_x_second(pz) for pz in CHUNKS[1]])
    turn(1)
    inward(2)
    on_core(0, lambda: ring_z(1))
    on_core(1, lambda: ([rows_x_first(pz) for pz in CHUNKS[2]], line_z_first()))
    relay_y(3)
    turn(2)
    on_core(1, lambda: [rows_x_second(pz) for pz in CHUNKS[2]])
    inward(3)
    on_core(0, lambda: ring_z(2))
    on_core(1, lambda: ([rows_x_first(pz) for pz in CHUNKS[3]], line_z(1)))
    turn(3)
    on_core(1, lambda: [rows_x_second(pz) for pz in CHUNKS[3]])
    weights_some(3)
    on_core(0, lambda: ring_z(3))
    on_core(1, lambda: line_z(2))
    weights_some(3)
    on_core(0, lambda: (ring_z_last(), line_x_first()))
    on_core(1, lambda: line_z(3))
    weights_some(2)
    on_core(0, line_x_second)
    on_core(1, line_z_last)
    weights_some(2)
    last()
    weights_some(12)
    for copy in started[None]:
        sent(*copy)
    for number in range(2):
        on_core(number, lambda: [sent(*copy) for copy in started[number]])


def shards(inputs, up_weight, down_weight, cotangent):
    rows, width = inputs.shape
    units = up_weight.shape[1]
    seg = NX * rows
    half = width // 2
    vmem = pltpu.VMEM
    anywhere = pl.BlockSpec(memory_space=pl.ANY)
    whole = pl.BlockSpec(memory_space=pltpu.VMEM)
    return pl.pallas_call(
        kernel,
        out_shape=(
            jax.ShapeDtypeStruct((rows, width), bf16),
            jax.ShapeDtypeStruct((width, units), bf16),
            jax.ShapeDtypeStruct((units, width), bf16),
        ),
        in_specs=[anywhere] * 4,
        out_specs=(whole, whole, whole),
        scratch_shapes=[
            vmem((2, NZ, NX, 2, rows, width), bf16),
            vmem((width, units), bf16),
            vmem((units, width), bf16),
            vmem((4, 2, 4, seg, units), f32),
            vmem((4, 2, 4, seg, units), bf16),
            vmem((4, 2, 2, seg, units), bf16),
            vmem((4, 2, seg, units), bf16),
            vmem((4, 2, seg, units), bf16),
            vmem((4, 2, 4, seg, units), bf16),
            vmem((2, units, 16 * seg), bf16),
            vmem((NZ, NX, rows, width), f32),
            vmem((NZ, NX, rows, width), f32),
            vmem((NZ, NX, rows, width), f32),
            vmem((2, 4, NX, rows, width), bf16),
            vmem((2, 4, NX, rows, width), bf16),
            vmem((2, NZ, rows, half), bf16),
            vmem((2, NZ, rows, half), bf16),
            vmem((2, NZ, rows, width), bf16),
            vmem((2, NZ, rows, width), bf16),
            vmem((2, 3, rows, width), bf16),
            vmem((2, 3, rows, width), bf16),
            vmem((2, rows, width), f32),
            vmem((2, rows, width), f32),
            pltpu.SemaphoreType.DMA((4,)),
            pltpu.SemaphoreType.DMA((240,)),
            pltpu.SemaphoreType.DMA((240,)),
        ],
        compiler_params=pltpu.CompilerParams(
            collective_id=0, has_side_effects=True, vmem_limit_bytes=60 << 20
        ),
    )(inputs, cotangent, up_weight, down_weight)


def solution(mesh):
    torus = Mesh(mesh.devices.reshape(2, NZ, NX, NY), ("dp", "z", "x", "y"))
    return jax.shard_map(
        shards,
        mesh=torus,
        in_specs=(P(DP_ROW, "y"), P("y", DP_ROW), P(DP_ROW, "y"), P(DP_ROW, "y")),
        out_specs=(P(DP_ROW, "y"), P("y", DP_ROW), P(DP_ROW, "y")),
        check_vma=False,
    )
```

```python
import functools
import math

import jax
import jax.numpy as jnp
from jax import lax
from jax.experimental import pallas as pl
from jax.experimental.pallas import tpu as pltpu
from jax.sharding import Mesh
from jax.sharding import PartitionSpec as P

NZ, NX, NY = 8, 4, 4
DP_ROW = ("dp", "z", "x")
MESH = pl.DeviceIdType.MESH

ORDER = (
    (
        0, 4, 2, 1, 5, 3, 6, 12, 11, 32, 26, 7, 25, 18, 19, 42, 33, 14, 34, 8, 13, 28, 102, 43,
        9, 27, 44, 35, 20, 21, 52, 16, 92, 15, 103, 45, 104, 36, 10, 30, 37, 29, 23, 53, 62, 22, 54, 94,
        17, 93, 47, 31, 46, 105, 24, 63, 82, 38, 40, 55, 64, 39, 72, 95, 48, 107, 49, 106, 83, 84, 57, 56,
        41, 50, 74, 65, 73, 97, 96, 108, 110, 109, 85, 58, 51, 66, 67, 59, 75, 98, 100, 99, 87, 113, 114, 86,
        111, 68, 60, 76, 77, 69, 115, 116, 117, 118, 101, 70, 88, 90, 89, 78, 80, 79, 119, 120, 121, 61, 122, 123,
        124, 71, 91, 81, 112,
    ),
    (
        0, 26, 2, 1, 25, 5, 4, 28, 3, 32, 27, 22, 23, 6, 8, 34, 7, 33, 30, 20, 42, 19, 24, 102,
        29, 35, 9, 43, 11, 10, 44, 21, 104, 103, 92, 36, 37, 17, 31, 52, 16, 45, 12, 105, 94, 93, 62, 14,
        53, 13, 54, 38, 18, 39, 82, 46, 47, 106, 107, 15, 72, 95, 63, 64, 55, 83, 84, 40, 48, 49, 50, 73,
        74, 108, 109, 96, 97, 41, 65, 57, 56, 85, 51, 75, 98, 99, 113, 66, 67, 110, 114, 86, 87, 115, 77, 58,
        60, 76, 59, 116, 117, 100, 118, 68, 111, 88, 70, 78, 79, 89, 69, 119, 61, 120, 121, 122, 90, 123, 101, 80,
        124, 71, 91, 81, 112,
    ),
)
RECORD = None
COPIES = 193
PIECE = 512
HALVES = ((0, 7, 1, 6), (2, 3, 5, 4))

gelu_const = math.sqrt(2.0 / math.pi)
bf16, f32 = jnp.bfloat16, jnp.float32


def gelu_and_slope(value):
    tangent = jnp.tanh(gelu_const * (value + 0.044715 * value * value * value))
    half = 0.5 * (1.0 + tangent)
    slope = half + 0.5 * value * (1.0 - tangent * tangent) * gelu_const * (
        1.0 + 3.0 * 0.044715 * value * value
    )
    return value * half, slope


def contract(left, right, dims):
    return lax.dot_general(left, right, ((dims[:1], dims[1:]), ((), ())), preferred_element_type=f32)


class at:
    def __init__(self, ref):
        self.ref, self.index = ref, ()

    def __getitem__(self, index):
        self.index = index
        return self

    def __call__(self):
        return self.ref.at[self.index]


class Names:
    def __init__(self):
        self.known = {}

    def __call__(self, name):
        return self.known.setdefault(name, len(self.known))


def kernel(
    x_hbm, g_hbm, wu_hbm, wd_hbm, dx_out, up_out, down_out,
    XG, WU, WD, PART, PART16, R1, S2, R2, AD, AT, Q, PS, PR,
    XS, XR, ZS, ZR, ACC, local_sem, send_sem, recv_sem,
):
    width, units = WU.shape
    piece = ACC.shape[3]
    core, z, x, y = (lax.axis_index(a) for a in ("dp", "z", "x", "y"))
    partner = {"dp": 1 - core}
    left_z, right_z = {"z": (z + NZ - 1) % NZ}, {"z": (z + 1) % NZ}
    left_x, right_x = {"x": (x + NX - 1) % NX}, {"x": (x + 1) % NX}
    ya = y + 1 - 2 * (y % 2)
    yb = 3 - y
    yab = 3 - ya
    near_a, near_b = {"y": ya}, {"y": yb}
    away_x = [{"x": (x + d) % NX} for d in range(NX)]
    away_z = [{"z": (z + d) % NZ} for d in range(NZ)]
    links = {id(partner): "p", id(left_z): "z-", id(right_z): "z+", id(left_x): "x-", id(right_x): "x+"}
    links.update({id(near_a): "a", id(near_b): "b"})
    links.update({id(device): ("z", d) for d, device in enumerate(away_z)})
    links.update({id(device): ("x", d) for d, device in enumerate(away_x)})
    names = Names()

    def log(kind, *what):
        if RECORD is not None:
            RECORD.append((kind, *what))

    def send(src, dst, device, name, group):
        log("send", links[id(device)], name, math.prod(src().shape) * src().dtype.itemsize)
        pltpu.make_async_remote_copy(
            src_ref=src(),
            dst_ref=dst(),
            send_sem=send_sem.at[group],
            recv_sem=recv_sem.at[names(name)],
            device_id=device,
            device_id_type=MESH,
        ).start()

    def recv(dst, name):
        log("recv", name)
        pltpu.make_async_remote_copy(
            src_ref=dst(),
            dst_ref=dst(),
            send_sem=send_sem.at[0],
            recv_sem=recv_sem.at[names(name)],
            device_id=partner,
            device_id_type=MESH,
        ).wait_recv()

    def sent(src, group):
        pltpu.make_async_remote_copy(
            src_ref=src(),
            dst_ref=src(),
            send_sem=send_sem.at[group],
            recv_sem=recv_sem.at[0],
            device_id=partner,
            device_id_type=MESH,
        ).wait_send()

    barrier = pltpu.get_barrier_semaphore()
    near = (partner, left_z, right_z, left_x, right_x, near_a, near_b)
    for device in near:
        pl.semaphore_signal(barrier, inc=1, device_id=device, device_id_type=MESH)
    local = [
        pltpu.make_async_copy(src, dst, local_sem.at[k])
        for k, (src, dst) in enumerate(
            ((x_hbm, XG.at[0, 0, 0, 0]), (g_hbm, XG.at[0, 0, 0, 1]), (wu_hbm, WU), (wd_hbm, WD))
        )
    ]
    for copy in local:
        copy.start()
    pl.semaphore_wait(barrier, len(near))
    local[0].wait()
    local[1].wait()

    def hand(pz_from, pz_to, px_from, px_to, device, a=None):
        group = 0 if px_from == px_to else 1
        if a is None:
            src, dst = at(XG)[0, pz_from, px_from], at(XG)[0, pz_to, px_to]
        else:
            src, dst = at(XG)[0, pz_from, px_from, a], at(XG)[0, pz_to, px_to, a]
        send(src, dst, device, ("xg", pz_to, px_to, a), group)

    def get(pz, px, a=None):
        recv(at(XG)[0, pz, px] if a is None else at(XG)[0, pz, px, a], ("xg", pz, px, a))

    def spread_z(px):
        hand(0, NZ - 1, px, px, right_z)
        hand(0, 1, px, px, left_z)

    def spread_x(pz):
        hand(pz, pz, 0, NX - 1, right_x)
        hand(pz, pz, 0, 1, left_x)

    def pair(pz, px):
        send(at(XG)[0, pz, px], at(XG)[1, pz, px], partner, ("pair", pz), 2)

    def begin():
        spread_x(0)
        spread_z(0)
        pair(0, 0)

    def step_x(pz, s, then):
        px = (3, 1)[s]
        get(pz, px)
        hand(pz, pz, px, 2, (right_x, left_x)[s], s)
        then(pz, px)
        pair(pz, px)

    def end_x(pz, then):
        get(pz, 2, 0)
        get(pz, 2, 1)
        then(pz, 2)
        pair(pz, 2)

    def step_z(d, px, s, then):
        pz = (NZ - d, d)[s]
        get(pz, px)
        beyond = pz - 1 if s == 0 else pz + 1
        hand(pz, beyond, px, px, (right_z, left_z)[s], s if beyond == 4 else None)
        then(pz, px)
        pair(pz, px)

    def end_z(px, then):
        get(4, px, 0)
        get(4, px, 1)
        then(4, px)
        pair(4, px)

    def nothing(pz, px):
        pass

    def along_z(pz, px):
        spread_z(px)

    def along_x(pz, px):
        spread_x(pz)

    def tokens(pz, a, columns=slice(None)):
        return [XG[k, pz, :, a, :, columns].reshape(NX * 16, -1) for k in range(2)]

    def products(pz):
        recv(at(XG)[1, pz], ("pair", pz))
        for a, (weights, dims) in enumerate(((WU, (1, 0)), (WD, (1, 1)))):
            part = contract(jnp.concatenate(tokens(pz, a), axis=0), weights[...], dims)
            part = part.reshape(4, NX * 8, units)
            PART[pz, a] = part
            PART16[pz, a] = part.astype(bf16)
        for k in (1, 0):
            for a, device, first in ((0, near_a, ya), (1, near_b, yb)):
                owner = yab if k else first
                send(at(PART16)[pz, a, owner], at(R1)[pz, a, k], device, ("r1", pz, a, k), 3)

    def second(pz, a):
        device, owner = ((near_b, yb), (near_a, ya))[a]
        recv(at(R1)[pz, a, 1], ("r1", pz, a, 1))
        S2[pz, a] = (PART[pz, a, owner] + R1[pz, a, 1].astype(f32)).astype(bf16)
        send(at(S2)[pz, a], at(R2)[pz, a], device, ("r2", pz, a), 4)

    def activate(pz):
        sums = []
        for a in range(2):
            recv(at(R1)[pz, a, 0], ("r1", pz, a, 0))
            recv(at(R2)[pz, a], ("r2", pz, a))
            sums.append(PART[pz, a, y] + R1[pz, a, 0].astype(f32) + R2[pz, a].astype(f32))
        active, slope = gelu_and_slope(sums[0])
        AD[pz, 0, y] = active.astype(bf16)
        AD[pz, 1, y] = (sums[1] * slope).astype(bf16)
        for a, device, side in ((0, near_b, "b"), (1, near_a, "a"), (0, near_a, "a"), (1, near_b, "b")):
            send(at(AD)[pz, a, y], at(AD)[pz, a, y], device, ("ad", pz, a, side), 4)

    def pass_on(pz, a):
        owner, device = ((yb, near_a), (ya, near_b))[a]
        recv(at(AD)[pz, a, owner], ("ad", pz, a, "ba"[a]))
        send(at(AD)[pz, a, owner], at(AD)[pz, a, owner], device, ("ad", pz, a, "ab"), 4)

    def inward(pz):
        for a, owner in ((1, yb), (0, ya)):
            recv(at(AD)[pz, a, owner], ("ad", pz, a, "ab"[a]))
            recv(at(AD)[pz, a, yab], ("ad", pz, a, "ab"))
        delta = AD[pz, 1].reshape(8 * NX * 4, units)
        back = contract(delta, WU[...], (1, 1)).reshape(2, NX, 16, width)
        PS[pz] = back[1]
        send(at(PS)[pz], at(PR)[pz], partner, ("back", pz), 5)
        Q[pz] = back[0]

    def turn(pz):
        place = (HALVES[0] + HALVES[1]).index(pz)
        rows = slice(place * 8 * 16, (place + 1) * 8 * 16)
        for a in range(2):
            AT[a, :, rows] = AD[pz, a].reshape(8 * 16, units).T

    def rows(pz):
        recv(at(PR)[pz], ("back", pz))
        for px in (2, 1, 3):
            XS[pz, px - 1] = (Q[pz, px] + PR[pz, px]).astype(bf16)
            send(at(XS)[pz, px - 1], at(XR)[pz, px - 1], away_x[px], ("x", px, pz), 6)

    def rows_last(pz):
        value = Q[pz, 0] + PR[pz, 0]
        for px in (1, 3, 2):
            recv(at(XR)[pz, px - 1], ("x", px, pz))
            value = value + XR[pz, px - 1].astype(f32)
        if pz == 0:
            Q[0, 0] = value
        else:
            ZS[pz - 1] = value.astype(bf16)
            send(at(ZS)[pz - 1], at(ZR)[pz - 1], away_z[pz], ("z", pz), 7)

    def finish():
        value = Q[0, 0]
        for pz in range(1, NZ):
            recv(at(ZR)[pz - 1], ("z", pz))
            value = value + ZR[pz - 1].astype(f32)
        dx_out[...] = value.astype(bf16)

    def weights(n, a, part):
        columns = slice(n * piece, (n + 1) * piece)
        group = HALVES[part]
        every = jnp.concatenate([t for pz in group for t in tokens(pz, a, columns)], axis=0)
        low = part * 4 * 8 * 16
        grad = contract(AT[1 - a, :, low : low + 4 * 8 * 16], every, (1, 0))
        if part == 0:
            ACC[a, n] = grad
        elif a == 0:
            up_out[columns, :] = ((ACC[a, n] + grad) * 0.5).T.astype(bf16)
        else:
            down_out[:, columns] = ((ACC[a, n] + grad) * 0.5).astype(bf16)

    def tasks(number):
        every = {("begin",): (begin, ())}
        far, near_then, far_then = (
            ((0,), along_z, nothing) if number == 0 else (range(NZ), nothing, along_x)
        )
        for pz in far:
            for s in range(2):
                every["x", pz, s] = (functools.partial(step_x, pz, s, near_then), ())
            every["end_x", pz] = (functools.partial(end_x, pz, near_then), ())
        for px in range(NX) if number == 0 else (0,):
            for d in (1, 2, 3):
                for s in range(2):
                    every["z", d, px, s] = (functools.partial(step_z, d, px, s, far_then), ())
            every["end_z", px] = (functools.partial(end_z, px, far_then), ())
        for pz in range(NZ):
            own = [k for k in every if k[0] in ("x", "end_x") and k[1] == pz]
            if pz == 4:
                own += [k for k in every if k[0] == "end_z"]
            elif pz:
                own += [k for k in every if k[0] == "z" and (NZ - k[1], k[1])[k[3]] == pz]
            every["products", pz] = (functools.partial(products, pz), tuple(own))
            for a in range(2):
                every["second", pz, a] = (functools.partial(second, pz, a), (("products", pz),))
            every["activate", pz] = (functools.partial(activate, pz), (("products", pz),))
            for a in range(2):
                every["pass", pz, a] = (functools.partial(pass_on, pz, a), (("activate", pz),))
            passed = (("pass", pz, 0), ("pass", pz, 1))
            every["inward", pz] = (functools.partial(inward, pz), passed)
            every["turn", pz] = (functools.partial(turn, pz), (("inward", pz),))
            every["rows", pz] = (functools.partial(rows, pz), (("inward", pz),))
            every["rows3", pz] = (functools.partial(rows_last, pz), (("rows", pz),))
        every["finish",] = (finish, (("rows3", 0),))
        for part in range(2):
            turned = tuple(("turn", pz) for pz in HALVES[part])
            for a in range(2):
                for n in range(width // piece):
                    after = turned + ((("weights", n, a, 0),) if part else ())
                    every["weights", n, a, part] = (functools.partial(weights, n, a, part), after)
        return every

    def whole_core(number):
        @pl.when(core == number)
        def _():
            every = tasks(number)
            known = list(every)
            for step in ORDER[number] or range(len(known)):
                name = known[step]
                body, after = every.pop(name)
                log("task", number, name, after)
                if name[0] == "products" and not any(k[0] == "products" for k in done):
                    local[2].wait()
                    local[3].wait()
                done.append(name)
                scope(name, body)
            done.clear()
            if number == 0:
                sent(at(XG)[0, 1:8], 0)
                sent(at(XG)[0, 0, 1:4], 1)
            else:
                sent(at(XG)[0, 1:8, 0], 0)
                sent(at(XG)[0, :, 1:4], 1)
            for group, ref in ((2, XG.at[0]), (3, R1), (4, PART16), (5, PS), (6, XS), (7, ZS)):
                sent(lambda ref=ref: ref, group)

    def scope(name, body):
        body()

    done = []
    whole_core(0)
    whole_core(1)
    assert len(names.known) <= COPIES


def put_out(*refs):
    copies = [pltpu.make_async_copy(refs[k], refs[3 + k], refs[6].at[k]) for k in range(3)]
    for copy in copies:
        copy.start()
    for copy in copies:
        copy.wait()


def shards(inputs, up_weight, down_weight, cotangent):
    rows, width = inputs.shape
    units = up_weight.shape[1]
    seg = NX * rows // 2
    piece = min(PIECE, width)
    vmem = pltpu.VMEM
    anywhere = pl.BlockSpec(memory_space=pl.ANY)
    whole = pl.BlockSpec(memory_space=pltpu.VMEM)
    results = pl.pallas_call(
        kernel,
        out_shape=(
            pltpu.VMEM((rows, width), bf16),
            pltpu.VMEM((width, units), bf16),
            pltpu.VMEM((units, width), bf16),
        ),
        in_specs=[anywhere] * 4,
        out_specs=(whole, whole, whole),
        scratch_shapes=[
            vmem((2, NZ, NX, 2, rows, width), bf16),
            vmem((width, units), bf16),
            vmem((units, width), bf16),
            vmem((NZ, 2, 4, seg, units), f32),
            vmem((NZ, 2, 4, seg, units), bf16),
            vmem((NZ, 2, 2, seg, units), bf16),
            vmem((NZ, 2, seg, units), bf16),
            vmem((NZ, 2, seg, units), bf16),
            vmem((NZ, 2, 4, seg, units), bf16),
            vmem((2, units, NZ * 4 * seg), bf16),
            vmem((NZ, NX, rows, width), f32),
            vmem((NZ, NX, rows, width), f32),
            vmem((NZ, NX, rows, width), f32),
            vmem((NZ, NX - 1, rows, width), bf16),
            vmem((NZ, NX - 1, rows, width), bf16),
            vmem((NZ - 1, rows, width), bf16),
            vmem((NZ - 1, rows, width), bf16),
            vmem((2, width // piece, units, piece), f32),
            pltpu.SemaphoreType.DMA((4,)),
            pltpu.SemaphoreType.DMA((8,)),
            pltpu.SemaphoreType.DMA((COPIES,)),
        ],
        compiler_params=pltpu.CompilerParams(
            collective_id=0, has_side_effects=True, vmem_limit_bytes=52 << 20
        ),
    )(inputs, cotangent, up_weight, down_weight)
    return pl.pallas_call(
        put_out,
        out_shape=tuple(jax.ShapeDtypeStruct(r.shape, r.dtype) for r in results),
        in_specs=[whole] * 3,
        out_specs=(anywhere,) * 3,
        scratch_shapes=[pltpu.SemaphoreType.DMA((3,))],
        compiler_params=pltpu.CompilerParams(vmem_limit_bytes=4 << 20),
    )(*results)


def solution(mesh):
    torus = Mesh(mesh.devices.reshape(2, NZ, NX, NY), ("dp", "z", "x", "y"))
    return jax.shard_map(
        shards,
        mesh=torus,
        in_specs=(P(DP_ROW, "y"), P("y", DP_ROW), P(DP_ROW, "y"), P(DP_ROW, "y")),
        out_specs=(P(DP_ROW, "y"), P("y", DP_ROW), P(DP_ROW, "y")),
        check_vma=False,
    )
```

```python
import functools
import math

import jax
import jax.numpy as jnp
from jax import lax
from jax.experimental import pallas as pl
from jax.experimental.pallas import tpu as pltpu
from jax.sharding import Mesh
from jax.sharding import PartitionSpec as P

NZ, NX, NY = 8, 4, 4
DP_ROW = ("dp", "z", "x")
MESH = pl.DeviceIdType.MESH

ORDER = (
    (
        0, 1, 8, 2, 7, 3, 32, 25, 26, 10, 13, 14, 9, 33, 34, 19, 20, 42, 102, 28, 27, 12, 35, 15,
        43, 44, 11, 16, 104, 103, 22, 52, 37, 21, 36, 30, 29, 45, 105, 17, 31, 92, 18, 53, 54, 38, 47, 23,
        24, 39, 46, 82, 107, 106, 4, 5, 94, 93, 40, 55, 62, 48, 83, 84, 6, 49, 108, 109, 95, 72, 41, 56,
        57, 73, 74, 63, 64, 50, 85, 96, 97, 110, 75, 58, 51, 59, 65, 113, 111, 86, 87, 114, 115, 98, 99, 116,
        117, 60, 76, 118, 77, 78, 66, 67, 79, 100, 88, 89, 68, 61, 80, 69, 90, 119, 120, 121, 101, 122, 123, 124,
        70, 81, 91, 71, 112,
    ),
    (
        0, 2, 1, 26, 25, 3, 4, 5, 32, 22, 23, 28, 27, 6, 34, 33, 24, 8, 7, 42, 29, 30, 19, 20,
        102, 35, 9, 44, 43, 16, 17, 31, 104, 103, 52, 37, 36, 21, 10, 11, 45, 92, 105, 18, 14, 13, 53, 54,
        12, 38, 40, 46, 47, 39, 82, 93, 94, 15, 106, 107, 55, 62, 48, 41, 50, 83, 84, 95, 49, 108, 110, 109,
        72, 56, 57, 73, 74, 64, 63, 85, 51, 96, 97, 111, 75, 58, 65, 60, 59, 87, 113, 86, 114, 115, 98, 99,
        100, 116, 117, 76, 77, 118, 67, 78, 61, 66, 80, 88, 89, 79, 90, 101, 68, 70, 69, 119, 120, 81, 121, 122,
        123, 91, 124, 71, 112,
    ),
)
RECORD = None
COPIES = 150
DIRECT = (4,)
PIECE = 512
HALVES = ((0, 1, 7, 2), (6, 5, 3, 4))

gelu_const = math.sqrt(2.0 / math.pi)
bf16, f32 = jnp.bfloat16, jnp.float32


def gelu_and_slope(value):
    tangent = jnp.tanh(gelu_const * (value + 0.044715 * value * value * value))
    half = 0.5 * (1.0 + tangent)
    slope = half + 0.5 * value * (1.0 - tangent * tangent) * gelu_const * (
        1.0 + 3.0 * 0.044715 * value * value
    )
    return value * half, slope


def contract(left, right, dims):
    return lax.dot_general(left, right, ((dims[:1], dims[1:]), ((), ())), preferred_element_type=f32)


class at:
    def __init__(self, ref):
        self.ref, self.index = ref, ()

    def __getitem__(self, index):
        self.index = index
        return self

    def __call__(self):
        return self.ref.at[self.index]


class Names:
    def __init__(self):
        self.known = {}

    def __call__(self, name):
        return self.known.setdefault(name, len(self.known))


def kernel(
    x_hbm, g_hbm, wu_hbm, wd_hbm, dx_out, up_out, down_out,
    XG, WU, WD, PART, PART16, IN, S2, AD, AT, Q, PS, PR,
    XS, XR, ZS, ZR, ACC, local_sem, send_sem, recv_sem,
):
    width, units = WU.shape
    piece = ACC.shape[3]
    core, z, x, y = (lax.axis_index(a) for a in ("dp", "z", "x", "y"))
    partner = {"dp": 1 - core}
    left_z, right_z = {"z": (z + NZ - 1) % NZ}, {"z": (z + 1) % NZ}
    left_x, right_x = {"x": (x + NX - 1) % NX}, {"x": (x + 1) % NX}
    ya = y + 1 - 2 * (y % 2)
    yb = 3 - y
    yab = 3 - ya
    near_a, near_b = {"y": ya}, {"y": yb}
    away_y = {"y": yab}
    away_x = [{"x": (x + d) % NX} for d in range(NX)]
    away_z = [{"z": (z + d) % NZ} for d in range(NZ)]
    links = {id(partner): "p", id(left_z): "z-", id(right_z): "z+", id(left_x): "x-", id(right_x): "x+"}
    links.update({id(near_a): "a", id(near_b): "b", id(away_y): ("y", 2)})
    links.update({id(device): ("z", d) for d, device in enumerate(away_z)})
    links.update({id(device): ("x", d) for d, device in enumerate(away_x)})
    names = Names()

    def log(kind, *what):
        if RECORD is not None:
            RECORD.append((kind, *what))

    def send(src, dst, device, name, group):
        log("send", links[id(device)], name, math.prod(src().shape) * src().dtype.itemsize)
        pltpu.make_async_remote_copy(
            src_ref=src(),
            dst_ref=dst(),
            send_sem=send_sem.at[group],
            recv_sem=recv_sem.at[names(name)],
            device_id=device,
            device_id_type=MESH,
        ).start()

    def recv(dst, name):
        log("recv", name)
        pltpu.make_async_remote_copy(
            src_ref=dst(),
            dst_ref=dst(),
            send_sem=send_sem.at[0],
            recv_sem=recv_sem.at[names(name)],
            device_id=partner,
            device_id_type=MESH,
        ).wait_recv()

    def sent(src, group):
        pltpu.make_async_remote_copy(
            src_ref=src(),
            dst_ref=src(),
            send_sem=send_sem.at[group],
            recv_sem=recv_sem.at[0],
            device_id=partner,
            device_id_type=MESH,
        ).wait_send()

    barrier = pltpu.get_barrier_semaphore()
    near = (partner, left_z, right_z, left_x, right_x, away_x[2], near_a, near_b)
    for device in near:
        pl.semaphore_signal(barrier, inc=1, device_id=device, device_id_type=MESH)
    local = [
        pltpu.make_async_copy(src, dst, local_sem.at[k])
        for k, (src, dst) in enumerate(
            ((x_hbm, XG.at[0, 0, 0, 0]), (g_hbm, XG.at[0, 0, 0, 1]), (wu_hbm, WU), (wd_hbm, WD))
        )
    ]
    for copy in local:
        copy.start()
    pl.semaphore_wait(barrier, len(near))
    local[0].wait()
    local[1].wait()

    def hand(pz_from, pz_to, px_from, px_to, device, a=None):
        group = 1 if px_from != px_to else 8 if pz_to == 4 else 0
        if a is None:
            src, dst = at(XG)[0, pz_from, px_from], at(XG)[0, pz_to, px_to]
        else:
            src, dst = at(XG)[0, pz_from, px_from, a], at(XG)[0, pz_to, px_to, a]
        send(src, dst, device, ("xg", pz_to, px_to, a), group)

    def get(pz, px, a=None):
        recv(at(XG)[0, pz, px] if a is None else at(XG)[0, pz, px, a], ("xg", pz, px, a))

    def spread_z(px):
        hand(0, NZ - 1, px, px, right_z)
        hand(0, 1, px, px, left_z)

    def spread_x(pz):
        hand(pz, pz, 0, NX - 1, right_x)
        hand(pz, pz, 0, 1, left_x)
        if pz == 0:
            hand(pz, pz, 0, 2, away_x[2])

    def pair(pz, px):
        send(at(XG)[0, pz, px], at(XG)[1, pz, px], partner, ("pair", pz), 2)

    def begin():
        spread_x(0)
        spread_z(0)
        pair(0, 0)

    def step_x(pz, s, then):
        px = (3, 1)[s]
        get(pz, px)
        if pz:
            hand(pz, pz, px, 2, (right_x, left_x)[s], s)
        then(pz, px)
        pair(pz, px)

    def end_x(pz, then):
        if pz:
            get(pz, 2, 0)
            get(pz, 2, 1)
        else:
            get(pz, 2)
        then(pz, 2)
        pair(pz, 2)

    def step_z(d, px, s, then):
        pz = (NZ - d, d)[s]
        get(pz, px)
        beyond = pz - 1 if s == 0 else pz + 1
        if beyond != 4 or px == 0:
            hand(pz, beyond, px, px, (right_z, left_z)[s], s if beyond == 4 else None)
        then(pz, px)
        pair(pz, px)

    def end_z(px, then):
        get(4, px, 0)
        get(4, px, 1)
        then(4, px)
        pair(4, px)

    def nothing(pz, px):
        pass

    def along_z(pz, px):
        spread_z(px)

    def along_x(pz, px):
        spread_x(pz)

    def tokens(pz, a, columns=slice(None)):
        return [XG[k, pz, :, a, :, columns].reshape(NX * 16, -1) for k in range(2)]

    def products(pz):
        recv(at(XG)[1, pz], ("pair", pz))
        for a, (weights, dims) in enumerate(((WU, (1, 0)), (WD, (1, 1)))):
            part = contract(jnp.concatenate(tokens(pz, a), axis=0), weights[...], dims)
            part = part.reshape(4, NX * 8, units)
            PART[pz, a] = part
            PART16[pz, a] = part.astype(bf16)
        ways = ((near_a, ya), (near_b, yb), (away_y, yab))
        if pz in DIRECT:
            for k in (2, 0, 1):
                for a in range(2):
                    src = at(PART16)[pz, a, ways[k][1]]
                    send(src, at(IN)[pz, a, k], ways[k][0], ("in", pz, a), 4 if k == 2 else 3)
            return
        for a in range(2):
            send(at(PART16)[pz, a, yab], at(IN)[pz, a, 2], ways[a][0], ("half", pz, a), 3)
        for a in range(2):
            send(at(PART16)[pz, a, ways[a][1]], at(IN)[pz, a, 0], ways[a][0], ("in", pz, a), 3)

    def second(pz, a):
        device, owner = ((near_b, yb), (near_a, ya))[a]
        recv(at(IN)[pz, a, 2], ("half", pz, a))
        S2[pz, a] = (PART[pz, a, owner] + IN[pz, a, 2].astype(f32)).astype(bf16)
        send(at(S2)[pz, a], at(IN)[pz, a, 1], device, ("in", pz, a), 4)

    def activate(pz):
        sums = []
        parts = 3 if pz in DIRECT else 2
        for a in range(2):
            recv(at(IN)[pz, a, :parts], ("in", pz, a))
            value = PART[pz, a, y]
            for k in range(parts):
                value = value + IN[pz, a, k].astype(f32)
            sums.append(value)
        active, slope = gelu_and_slope(sums[0])
        AD[pz, 0, y] = active.astype(bf16)
        AD[pz, 1, y] = (sums[1] * slope).astype(bf16)
        own = [at(AD)[pz, a, y] for a in range(2)]
        if pz in DIRECT:
            for a in (1, 0):
                send(own[a], own[a], away_y, ("ad", pz, a, "ab"), 4)
        for a, device, side in ((0, near_b, "b"), (1, near_a, "a"), (0, near_a, "a"), (1, near_b, "b")):
            send(own[a], own[a], device, ("ad", pz, a, side), 4)

    def pass_on(pz, a):
        owner, device = ((yb, near_a), (ya, near_b))[a]
        recv(at(AD)[pz, a, owner], ("ad", pz, a, "ba"[a]))
        if pz not in DIRECT:
            send(at(AD)[pz, a, owner], at(AD)[pz, a, owner], device, ("ad", pz, a, "ab"), 4)

    def inward(pz):
        for a, owner in ((1, yb), (0, ya)):
            recv(at(AD)[pz, a, owner], ("ad", pz, a, "ab"[a]))
            recv(at(AD)[pz, a, yab], ("ad", pz, a, "ab"))
        delta = AD[pz, 1].reshape(8 * NX * 4, units)
        back = contract(delta, WU[...], (1, 1)).reshape(2, NX, 16, width)
        PS[pz] = back[1]
        send(at(PS)[pz], at(PR)[pz], partner, ("back", pz), 5)
        Q[pz] = back[0]

    def turn(pz):
        place = (HALVES[0] + HALVES[1]).index(pz)
        rows = slice(place * 8 * 16, (place + 1) * 8 * 16)
        for a in range(2):
            AT[a, :, rows] = AD[pz, a].reshape(8 * 16, units).T

    def rows(pz):
        recv(at(PR)[pz], ("back", pz))
        for px in (2, 1, 3):
            XS[pz, px - 1] = (Q[pz, px] + PR[pz, px]).astype(bf16)
            send(at(XS)[pz, px - 1], at(XR)[pz, px - 1], away_x[px], ("x", pz), 6)

    def rows_last(pz):
        value = Q[pz, 0] + PR[pz, 0]
        recv(at(XR)[pz], ("x", pz))
        for px in (1, 3, 2):
            value = value + XR[pz, px - 1].astype(f32)
        if pz == 0:
            Q[0, 0] = value
        else:
            ZS[pz - 1] = value.astype(bf16)
            send(at(ZS)[pz - 1], at(ZR)[pz - 1], away_z[pz], ("z",), 7)

    def finish():
        value = Q[0, 0]
        recv(lambda: ZR, ("z",))
        for pz in range(1, NZ):
            value = value + ZR[pz - 1].astype(f32)
        dx_out[...] = value.astype(bf16)

    def weights(n, a, part):
        columns = slice(n * piece, (n + 1) * piece)
        group = HALVES[part]
        every = jnp.concatenate([t for pz in group for t in tokens(pz, a, columns)], axis=0)
        low = part * 4 * 8 * 16
        grad = contract(AT[1 - a, :, low : low + 4 * 8 * 16], every, (1, 0))
        if part == 0:
            ACC[a, n] = grad
        elif a == 0:
            up_out[columns, :] = ((ACC[a, n] + grad) * 0.5).T.astype(bf16)
        else:
            down_out[:, columns] = ((ACC[a, n] + grad) * 0.5).astype(bf16)

    def tasks(number):
        every = {("begin",): (begin, ())}
        for pz in (0, 4) if number == 0 else range(NZ):
            then = along_z if number == 0 and pz == 0 else nothing
            for s in range(2):
                every["x", pz, s] = (functools.partial(step_x, pz, s, then), ())
            every["end_x", pz] = (functools.partial(end_x, pz, then), ())
        for px in range(NX) if number == 0 else (0,):
            for d in (1, 2, 3):
                for s in range(2):
                    then = along_x if number == 1 else nothing
                    every["z", d, px, s] = (functools.partial(step_z, d, px, s, then), ())
        every["end_z", 0] = (functools.partial(end_z, 0, along_x), ())
        for pz in range(NZ):
            own = [k for k in every if k[0] in ("x", "end_x") and k[1] == pz]
            if pz == 4:
                own += [k for k in every if k[0] == "end_z"]
            elif pz:
                own += [k for k in every if k[0] == "z" and (NZ - k[1], k[1])[k[3]] == pz]
            every["products", pz] = (functools.partial(products, pz), tuple(own))
            for a in range(2):
                step = (lambda: None) if pz in DIRECT else functools.partial(second, pz, a)
                every["second", pz, a] = (step, (("products", pz),))
            every["activate", pz] = (functools.partial(activate, pz), (("products", pz),))
            for a in range(2):
                every["pass", pz, a] = (functools.partial(pass_on, pz, a), (("activate", pz),))
            passed = (("pass", pz, 0), ("pass", pz, 1))
            every["inward", pz] = (functools.partial(inward, pz), passed)
            every["turn", pz] = (functools.partial(turn, pz), (("inward", pz),))
            every["rows", pz] = (functools.partial(rows, pz), (("inward", pz),))
            every["rows3", pz] = (functools.partial(rows_last, pz), (("rows", pz),))
        every["finish",] = (finish, (("rows3", 0),))
        for part in range(2):
            turned = tuple(("turn", pz) for pz in HALVES[part])
            for a in range(2):
                for n in range(width // piece):
                    after = turned + ((("weights", n, a, 0),) if part else ())
                    every["weights", n, a, part] = (functools.partial(weights, n, a, part), after)
        return every

    def whole_core(number):
        @pl.when(core == number)
        def _():
            every = tasks(number)
            known = list(every)
            for step in ORDER[number] or range(len(known)):
                name = known[step]
                body, after = every.pop(name)
                log("task", number, name, after)
                if name[0] == "products" and not any(k[0] == "products" for k in done):
                    local[2].wait()
                    local[3].wait()
                done.append(name)
                scope(name, body)
            done.clear()
            if number == 0:
                sent(at(XG)[0, 1:7], 0)
                sent(at(XG)[0, 1:3, 1:4], 1)
            else:
                sent(at(XG)[0, 1:7, 0], 0)
                sent(at(XG)[0, :, 1:4], 1)
            sent(at(XG)[0, 4, 0], 8)
            for group, ref in ((2, XG.at[0]), (3, PART16.at[:, 0]), (4, PART16), (5, PS), (6, XS), (7, ZS)):
                sent(lambda ref=ref: ref, group)

    def scope(name, body):
        body()

    done = []
    whole_core(0)
    whole_core(1)
    assert len(names.known) <= COPIES


def put_out(*refs):
    copies = [pltpu.make_async_copy(refs[k], refs[3 + k], refs[6].at[k]) for k in range(3)]
    for copy in copies:
        copy.start()
    for copy in copies:
        copy.wait()


def shards(inputs, up_weight, down_weight, cotangent):
    rows, width = inputs.shape
    units = up_weight.shape[1]
    seg = NX * rows // 2
    piece = min(PIECE, width)
    vmem = pltpu.VMEM
    anywhere = pl.BlockSpec(memory_space=pl.ANY)
    whole = pl.BlockSpec(memory_space=pltpu.VMEM)
    results = pl.pallas_call(
        kernel,
        out_shape=(
            pltpu.VMEM((rows, width), bf16),
            pltpu.VMEM((width, units), bf16),
            pltpu.VMEM((units, width), bf16),
        ),
        in_specs=[anywhere] * 4,
        out_specs=(whole, whole, whole),
        scratch_shapes=[
            vmem((2, NZ, NX, 2, rows, width), bf16),
            vmem((width, units), bf16),
            vmem((units, width), bf16),
            vmem((NZ, 2, 4, seg, units), f32),
            vmem((NZ, 2, 4, seg, units), bf16),
            vmem((NZ, 2, 3, seg, units), bf16),
            vmem((NZ, 2, seg, units), bf16),
            vmem((NZ, 2, 4, seg, units), bf16),
            vmem((2, units, NZ * 4 * seg), bf16),
            vmem((NZ, NX, rows, width), f32),
            vmem((NZ, NX, rows, width), f32),
            vmem((NZ, NX, rows, width), f32),
            vmem((NZ, NX - 1, rows, width), bf16),
            vmem((NZ, NX - 1, rows, width), bf16),
            vmem((NZ - 1, rows, width), bf16),
            vmem((NZ - 1, rows, width), bf16),
            vmem((2, width // piece, units, piece), f32),
            pltpu.SemaphoreType.DMA((4,)),
            pltpu.SemaphoreType.DMA((9,)),
            pltpu.SemaphoreType.DMA((COPIES,)),
        ],
        compiler_params=pltpu.CompilerParams(
            collective_id=0, has_side_effects=True, vmem_limit_bytes=52 << 20
        ),
    )(inputs, cotangent, up_weight, down_weight)
    return pl.pallas_call(
        put_out,
        out_shape=tuple(jax.ShapeDtypeStruct(r.shape, r.dtype) for r in results),
        in_specs=[whole] * 3,
        out_specs=(anywhere,) * 3,
        scratch_shapes=[pltpu.SemaphoreType.DMA((3,))],
        compiler_params=pltpu.CompilerParams(vmem_limit_bytes=4 << 20),
    )(*results)


def solution(mesh):
    torus = Mesh(mesh.devices.reshape(2, NZ, NX, NY), ("dp", "z", "x", "y"))
    return jax.shard_map(
        shards,
        mesh=torus,
        in_specs=(P(DP_ROW, "y"), P("y", DP_ROW), P(DP_ROW, "y"), P(DP_ROW, "y")),
        out_specs=(P(DP_ROW, "y"), P("y", DP_ROW), P(DP_ROW, "y")),
        check_vma=False,
    )
```

```python
import functools
import math

import jax
import jax.numpy as jnp
from jax import lax
from jax.experimental import pallas as pl
from jax.experimental.pallas import tpu as pltpu
from jax.sharding import Mesh
from jax.sharding import PartitionSpec as P

NZ, NX, NY = 8, 4, 4
DP_ROW = ("dp", "z", "x")
MESH = pl.DeviceIdType.MESH

ORDER = (
    (
        0, 7, 1, 8, 2, 3, 9, 32, 10, 13, 26, 19, 25, 20, 14, 33, 40, 12, 28, 11, 88, 21, 41, 15,
        22, 27, 80, 16, 31, 34, 89, 48, 30, 42, 23, 24, 18, 35, 17, 56, 5, 29, 4, 81, 43, 90, 72, 36,
        6, 57, 82, 91, 44, 49, 64, 46, 73, 58, 83, 92, 50, 38, 65, 59, 74, 45, 94, 84, 51, 66, 86, 60,
        75, 62, 67, 52, 93, 95, 76, 53, 37, 61, 78, 68, 70, 47, 87, 98, 97, 77, 99, 63, 39, 102, 100, 79,
        54, 101, 71, 69, 85, 107, 105, 55, 108, 104, 103, 106, 96,
    ),
    (
        0, 26, 25, 4, 5, 2, 3, 1, 32, 27, 23, 22, 28, 6, 20, 19, 24, 33, 30, 88, 8, 7, 29, 40,
        34, 21, 11, 10, 31, 89, 9, 41, 80, 35, 90, 16, 42, 17, 12, 48, 13, 81, 14, 56, 18, 43, 72, 91,
        15, 57, 82, 36, 38, 64, 49, 44, 58, 73, 46, 83, 65, 59, 45, 50, 92, 94, 74, 84, 47, 66, 51, 60,
        37, 75, 86, 67, 61, 62, 52, 76, 95, 77, 54, 68, 63, 53, 69, 93, 70, 97, 85, 87, 78, 100, 39, 99,
        101, 55, 105, 102, 98, 108, 71, 107, 106, 104, 79, 103, 96,
    ),
)
RECORD = None
COPIES = 88
DIRECT = ()
PIECE = 512
HALVES = ((0, 1, 7, 2), (6, 3, 5, 4))

gelu_const = math.sqrt(2.0 / math.pi)
bf16, f32 = jnp.bfloat16, jnp.float32


def gelu_and_slope(value):
    tangent = jnp.tanh(gelu_const * (value + 0.044715 * value * value * value))
    half = 0.5 * (1.0 + tangent)
    slope = half + 0.5 * value * (1.0 - tangent * tangent) * gelu_const * (
        1.0 + 3.0 * 0.044715 * value * value
    )
    return value * half, slope


def contract(left, right, dims):
    return lax.dot_general(left, right, ((dims[:1], dims[1:]), ((), ())), preferred_element_type=f32)


class at:
    def __init__(self, ref):
        self.ref, self.index = ref, ()

    def __getitem__(self, index):
        self.index = index
        return self

    def __call__(self):
        return self.ref.at[self.index]


class Names:
    def __init__(self):
        self.known = {}

    def __call__(self, name):
        return self.known.setdefault(name, len(self.known))


def kernel(
    x_hbm, g_hbm, wu_hbm, wd_hbm, dx_out, up_out, down_out,
    XG, WU, WD, PART, PART16, IN, S2, AD, AT, Q, PS, PR,
    XS, XR, ZS, ZR, ACC, local_sem, send_sem, recv_sem,
):
    width, units = WU.shape
    piece = ACC.shape[3]
    core, z, x, y = (lax.axis_index(a) for a in ("dp", "z", "x", "y"))
    partner = {"dp": 1 - core}
    left_z, right_z = {"z": (z + NZ - 1) % NZ}, {"z": (z + 1) % NZ}
    left_x, right_x = {"x": (x + NX - 1) % NX}, {"x": (x + 1) % NX}
    ya = y + 1 - 2 * (y % 2)
    yb = 3 - y
    yab = 3 - ya
    near_a, near_b = {"y": ya}, {"y": yb}
    away_y = {"y": yab}
    away_x = [{"x": (x + d) % NX} for d in range(NX)]
    away_z = [{"z": (z + d) % NZ} for d in range(NZ)]
    links = {id(partner): "p", id(left_z): "z-", id(right_z): "z+", id(left_x): "x-", id(right_x): "x+"}
    links.update({id(near_a): "a", id(near_b): "b", id(away_y): ("y", 2)})
    links.update({id(device): ("z", d) for d, device in enumerate(away_z)})
    links.update({id(device): ("x", d) for d, device in enumerate(away_x)})
    names = Names()

    def log(kind, *what):
        if RECORD is not None:
            RECORD.append((kind, *what))

    def send(src, dst, device, name, group):
        log("send", links[id(device)], name, math.prod(src().shape) * src().dtype.itemsize)
        pltpu.make_async_remote_copy(
            src_ref=src(),
            dst_ref=dst(),
            send_sem=send_sem.at[group],
            recv_sem=recv_sem.at[names(name)],
            device_id=device,
            device_id_type=MESH,
        ).start()

    def recv(dst, name):
        log("recv", name)
        pltpu.make_async_remote_copy(
            src_ref=dst(),
            dst_ref=dst(),
            send_sem=send_sem.at[0],
            recv_sem=recv_sem.at[names(name)],
            device_id=partner,
            device_id_type=MESH,
        ).wait_recv()

    def sent(src, group):
        pltpu.make_async_remote_copy(
            src_ref=src(),
            dst_ref=src(),
            send_sem=send_sem.at[group],
            recv_sem=recv_sem.at[0],
            device_id=partner,
            device_id_type=MESH,
        ).wait_send()

    barrier = pltpu.get_barrier_semaphore()
    near = (partner, left_z, right_z, left_x, right_x, away_x[2], near_a, near_b)
    for device in near:
        pl.semaphore_signal(barrier, inc=1, device_id=device, device_id_type=MESH)
    local = [
        pltpu.make_async_copy(src, dst, local_sem.at[k])
        for k, (src, dst) in enumerate(
            ((x_hbm, XG.at[0, 0, 0, 0]), (g_hbm, XG.at[0, 0, 0, 1]), (wu_hbm, WU), (wd_hbm, WD))
        )
    ]
    for copy in local:
        copy.start()
    pl.semaphore_wait(barrier, len(near))
    local[0].wait()
    local[1].wait()

    def hand(pz_from, pz_to, px_from, px_to, device, a=None):
        group = 1 if px_from != px_to else 8 if pz_to == 4 else 0
        if a is None:
            src, dst = at(XG)[0, pz_from, px_from], at(XG)[0, pz_to, px_to]
        else:
            src, dst = at(XG)[0, pz_from, px_from, a], at(XG)[0, pz_to, px_to, a]
        send(src, dst, device, ("xg", pz_to, px_to), group)

    def get(pz, px):
        recv(at(XG)[0, pz, px], ("xg", pz, px))

    def spread_z(px):
        hand(0, NZ - 1, px, px, right_z)
        hand(0, 1, px, px, left_z)

    def spread_x(pz):
        hand(pz, pz, 0, NX - 1, right_x)
        hand(pz, pz, 0, 1, left_x)
        if pz == 0:
            hand(pz, pz, 0, 2, away_x[2])

    def pair(pz, px):
        send(at(XG)[0, pz, px], at(XG)[1, pz, px], partner, ("pair", pz), 2)

    def begin():
        spread_x(0)
        spread_z(0)
        pair(0, 0)

    def step_x(pz, s, then):
        px = (3, 1)[s]
        get(pz, px)
        if pz:
            hand(pz, pz, px, 2, (right_x, left_x)[s], s)
        then(pz, px)
        pair(pz, px)

    def end_x(pz, then):
        get(pz, 2)
        then(pz, 2)
        pair(pz, 2)

    def step_z(d, px, s, then):
        pz = (NZ - d, d)[s]
        get(pz, px)
        beyond = pz - 1 if s == 0 else pz + 1
        if beyond != 4 or px == 0:
            hand(pz, beyond, px, px, (right_z, left_z)[s], s if beyond == 4 else None)
        then(pz, px)
        pair(pz, px)

    def end_z(px, then):
        get(4, px)
        then(4, px)
        pair(4, px)

    def nothing(pz, px):
        pass

    def along_z(pz, px):
        spread_z(px)

    def along_x(pz, px):
        spread_x(pz)

    def tokens(pz, a, columns=slice(None)):
        return [XG[k, pz, :, a, :, columns].reshape(NX * 16, -1) for k in range(2)]

    def products(pz):
        recv(at(XG)[1, pz], ("pair", pz))
        for a, (weights, dims) in enumerate(((WU, (1, 0)), (WD, (1, 1)))):
            part = contract(jnp.concatenate(tokens(pz, a), axis=0), weights[...], dims)
            part = part.reshape(4, NX * 8, units)
            PART[pz, a] = part
            PART16[pz, a] = part.astype(bf16)
        ways = ((near_a, ya), (near_b, yb), (away_y, yab))
        if pz in DIRECT:
            for k in (2, 0, 1):
                for a in range(2):
                    src = at(PART16)[pz, a, ways[k][1]]
                    send(src, at(IN)[pz, a, k], ways[k][0], ("in", pz), 4 if k == 2 else 3)
            return
        for a in range(2):
            send(at(PART16)[pz, a, yab], at(IN)[pz, a, 2], ways[a][0], ("half", pz), 3)
        for a in range(2):
            send(at(PART16)[pz, a, ways[a][1]], at(IN)[pz, a, 0], ways[a][0], ("in", pz), 3)

    def second(pz):
        recv(at(IN)[pz, :, 2], ("half", pz))
        for a, device, owner in ((0, near_b, yb), (1, near_a, ya)):
            S2[pz, a] = (PART[pz, a, owner] + IN[pz, a, 2].astype(f32)).astype(bf16)
            send(at(S2)[pz, a], at(IN)[pz, a, 1], device, ("in", pz), 4)

    def activate(pz):
        parts = 3 if pz in DIRECT else 2
        recv(at(IN)[pz, :, :parts], ("in", pz))
        sums = []
        for a in range(2):
            value = PART[pz, a, y]
            for k in range(parts):
                value = value + IN[pz, a, k].astype(f32)
            sums.append(value)
        active, slope = gelu_and_slope(sums[0])
        AD[pz, 0, y] = active.astype(bf16)
        AD[pz, 1, y] = (sums[1] * slope).astype(bf16)
        own = [at(AD)[pz, a, y] for a in range(2)]
        if pz in DIRECT:
            for a in (1, 0):
                send(own[a], own[a], away_y, ("rest", pz), 4)
        for a, device in ((0, near_b), (1, near_a)):
            send(own[a], own[a], device, ("first", pz), 4)
        for a, device in ((0, near_a), (1, near_b)):
            send(own[a], own[a], device, ("rest", pz), 4)

    def pass_on(pz):
        recv(at(S2)[pz], ("first", pz))
        if pz not in DIRECT:
            for a, owner, device in ((0, yb, near_a), (1, ya, near_b)):
                send(at(AD)[pz, a, owner], at(AD)[pz, a, owner], device, ("rest", pz), 4)

    def inward(pz):
        recv(at(AD)[pz, 0], ("rest", pz))
        delta = AD[pz, 1].reshape(8 * NX * 4, units)
        back = contract(delta, WU[...], (1, 1)).reshape(2, NX, 16, width)
        PS[pz] = back[1]
        send(at(PS)[pz], at(PR)[pz], partner, ("back", pz), 5)
        Q[pz] = back[0]

    def turn(pz):
        place = (HALVES[0] + HALVES[1]).index(pz)
        rows = slice(place * 8 * 16, (place + 1) * 8 * 16)
        for a in range(2):
            AT[a, :, rows] = AD[pz, a].reshape(8 * 16, units).T

    def rows(pz):
        recv(at(PR)[pz], ("back", pz))
        for px in (2, 1, 3):
            XS[pz, px - 1] = (Q[pz, px] + PR[pz, px]).astype(bf16)
            send(at(XS)[pz, px - 1], at(XR)[pz, px - 1], away_x[px], ("x", pz), 6)

    def rows_last(pz):
        value = Q[pz, 0] + PR[pz, 0]
        recv(at(XR)[pz], ("x", pz))
        for px in (1, 3, 2):
            value = value + XR[pz, px - 1].astype(f32)
        if pz == 0:
            Q[0, 0] = value
        else:
            ZS[pz - 1] = value.astype(bf16)
            send(at(ZS)[pz - 1], at(ZR)[pz - 1], away_z[pz], ("z",), 7)

    def finish():
        value = Q[0, 0]
        recv(lambda: ZR, ("z",))
        for pz in range(1, NZ):
            value = value + ZR[pz - 1].astype(f32)
        dx_out[...] = value.astype(bf16)

    def weights(n, a, part):
        columns = slice(n * piece, (n + 1) * piece)
        group = HALVES[part]
        every = jnp.concatenate([t for pz in group for t in tokens(pz, a, columns)], axis=0)
        low = part * 4 * 8 * 16
        grad = contract(AT[1 - a, :, low : low + 4 * 8 * 16], every, (1, 0))
        if part == 0:
            ACC[a, n] = grad
        elif a == 0:
            up_out[columns, :] = ((ACC[a, n] + grad) * 0.5).T.astype(bf16)
        else:
            down_out[:, columns] = ((ACC[a, n] + grad) * 0.5).astype(bf16)

    def tasks(number):
        every = {("begin",): (begin, ())}
        for pz in (0, 4) if number == 0 else range(NZ):
            then = along_z if number == 0 and pz == 0 else nothing
            for s in range(2):
                every["x", pz, s] = (functools.partial(step_x, pz, s, then), ())
            every["end_x", pz] = (functools.partial(end_x, pz, then), ())
        for px in range(NX) if number == 0 else (0,):
            for d in (1, 2, 3):
                for s in range(2):
                    then = along_x if number == 1 else nothing
                    every["z", d, px, s] = (functools.partial(step_z, d, px, s, then), ())
        every["end_z", 0] = (functools.partial(end_z, 0, along_x), ())
        for pz in range(NZ):
            own = [k for k in every if k[0] in ("x", "end_x") and k[1] == pz]
            if pz == 4:
                own += [k for k in every if k[0] == "end_z"]
            elif pz:
                own += [k for k in every if k[0] == "z" and (NZ - k[1], k[1])[k[3]] == pz]
            every["products", pz] = (functools.partial(products, pz), tuple(own))
            step = (lambda: None) if pz in DIRECT else functools.partial(second, pz)
            every["second", pz] = (step, (("products", pz),))
            every["activate", pz] = (functools.partial(activate, pz), (("products", pz),))
            every["pass", pz] = (functools.partial(pass_on, pz), (("activate", pz),))
            every["inward", pz] = (functools.partial(inward, pz), (("pass", pz),))
            every["turn", pz] = (functools.partial(turn, pz), (("inward", pz),))
            every["rows", pz] = (functools.partial(rows, pz), (("inward", pz),))
            every["rows3", pz] = (functools.partial(rows_last, pz), (("rows", pz),))
        every["finish",] = (finish, (("rows3", 0),))
        for part in range(2):
            turned = tuple(("turn", pz) for pz in HALVES[part])
            for a in range(2):
                for n in range(width // piece):
                    after = turned + ((("weights", n, a, 0),) if part else ())
                    every["weights", n, a, part] = (functools.partial(weights, n, a, part), after)
        return every

    def whole_core(number):
        @pl.when(core == number)
        def _():
            every = tasks(number)
            known = list(every)
            for step in ORDER[number] or range(len(known)):
                name = known[step]
                body, after = every.pop(name)
                log("task", number, name, after)
                if name[0] == "products" and not any(k[0] == "products" for k in done):
                    local[2].wait()
                    local[3].wait()
                done.append(name)
                scope(name, body)
            done.clear()
            if number == 0:
                sent(at(XG)[0, 1:7], 0)
                sent(at(XG)[0, 1:3, 1:4], 1)
            else:
                sent(at(XG)[0, 1:7, 0], 0)
                sent(at(XG)[0, :, 1:4], 1)
            sent(at(XG)[0, 4, 0], 8)
            for group, ref in ((2, XG.at[0]), (3, PART16.at[:, 0]), (4, PART16), (5, PS), (6, XS), (7, ZS)):
                sent(lambda ref=ref: ref, group)

    def scope(name, body):
        body()

    done = []
    whole_core(0)
    whole_core(1)
    assert len(names.known) <= COPIES


def put_out(*refs):
    copies = [pltpu.make_async_copy(refs[0], refs[3], refs[6].at[0])]
    for k in (1, 2):
        rows = refs[k].shape[0] // 4
        for n in range(4):
            part = pl.ds(n * rows, rows)
            src, dst = refs[k].at[part], refs[3 + k].at[part]
            copies.append(pltpu.make_async_copy(src, dst, refs[6].at[len(copies)]))
    for copy in copies:
        copy.start()
    for copy in copies:
        copy.wait()


def shards(inputs, up_weight, down_weight, cotangent):
    rows, width = inputs.shape
    units = up_weight.shape[1]
    seg = NX * rows // 2
    piece = min(PIECE, width)
    vmem = pltpu.VMEM
    anywhere = pl.BlockSpec(memory_space=pl.ANY)
    whole = pl.BlockSpec(memory_space=pltpu.VMEM)
    results = pl.pallas_call(
        kernel,
        out_shape=(
            pltpu.VMEM((rows, width), bf16),
            pltpu.VMEM((width, units), bf16),
            pltpu.VMEM((units, width), bf16),
        ),
        in_specs=[anywhere] * 4,
        out_specs=(whole, whole, whole),
        scratch_shapes=[
            vmem((2, NZ, NX, 2, rows, width), bf16),
            vmem((width, units), bf16),
            vmem((units, width), bf16),
            vmem((NZ, 2, 4, seg, units), f32),
            vmem((NZ, 2, 4, seg, units), bf16),
            vmem((NZ, 2, 3, seg, units), bf16),
            vmem((NZ, 2, seg, units), bf16),
            vmem((NZ, 2, 4, seg, units), bf16),
            vmem((2, units, NZ * 4 * seg), bf16),
            vmem((NZ, NX, rows, width), f32),
            vmem((NZ, NX, rows, width), f32),
            vmem((NZ, NX, rows, width), f32),
            vmem((NZ, NX - 1, rows, width), bf16),
            vmem((NZ, NX - 1, rows, width), bf16),
            vmem((NZ - 1, rows, width), bf16),
            vmem((NZ - 1, rows, width), bf16),
            vmem((2, width // piece, units, piece), f32),
            pltpu.SemaphoreType.DMA((4,)),
            pltpu.SemaphoreType.DMA((9,)),
            pltpu.SemaphoreType.DMA((COPIES,)),
        ],
        compiler_params=pltpu.CompilerParams(
            collective_id=0, has_side_effects=True, vmem_limit_bytes=52 << 20
        ),
    )(inputs, cotangent, up_weight, down_weight)
    return pl.pallas_call(
        put_out,
        out_shape=tuple(jax.ShapeDtypeStruct(r.shape, r.dtype) for r in results),
        in_specs=[whole] * 3,
        out_specs=(anywhere,) * 3,
        scratch_shapes=[pltpu.SemaphoreType.DMA((9,))],
        compiler_params=pltpu.CompilerParams(vmem_limit_bytes=4 << 20),
    )(*results)


def solution(mesh):
    torus = Mesh(mesh.devices.reshape(2, NZ, NX, NY), ("dp", "z", "x", "y"))
    return jax.shard_map(
        shards,
        mesh=torus,
        in_specs=(P(DP_ROW, "y"), P("y", DP_ROW), P(DP_ROW, "y"), P(DP_ROW, "y")),
        out_specs=(P(DP_ROW, "y"), P("y", DP_ROW), P(DP_ROW, "y")),
        check_vma=False,
    )
```

```python
import functools
import math

import jax
import jax.numpy as jnp
from jax import lax
from jax.experimental import pallas as pl
from jax.experimental.pallas import tpu as pltpu
from jax.sharding import Mesh
from jax.sharding import PartitionSpec as P

NZ, NX, NY = 8, 4, 4
DP_ROW = ("dp", "z", "x")
MESH = pl.DeviceIdType.MESH

ORDER = (
    (
        0, 8, 2, 7, 1, 3, 32, 80, 10, 13, 9, 14, 33, 81, 25, 26, 20, 38, 19, 74, 122, 34, 15, 12,
        82, 11, 16, 39, 86, 28, 75, 27, 123, 35, 116, 22, 83, 44, 21, 68, 40, 17, 87, 124, 18, 76, 31, 36,
        37, 29, 117, 30, 84, 45, 92, 24, 50, 23, 69, 41, 62, 88, 85, 77, 128, 125, 110, 5, 118, 4, 46, 93,
        51, 98, 70, 42, 43, 63, 89, 78, 111, 126, 129, 104, 119, 127, 79, 47, 6, 56, 52, 94, 99, 71, 64, 90,
        130, 112, 91, 142, 105, 120, 121, 48, 57, 49, 53, 95, 100, 72, 65, 73, 132, 113, 131, 106, 58, 54, 55, 96,
        143, 101, 97, 145, 140, 146, 66, 114, 107, 147, 59, 148, 134, 133, 149, 150, 115, 102, 103, 67, 138, 141, 108, 60,
        61, 109, 151, 152, 153, 135, 154, 155, 156, 136, 139, 137, 144,
    ),
    (
        0, 2, 1, 25, 26, 3, 32, 80, 22, 23, 27, 28, 5, 4, 33, 81, 24, 74, 20, 19, 86, 8, 34, 122,
        29, 30, 7, 82, 6, 38, 75, 21, 68, 87, 35, 123, 83, 17, 31, 16, 39, 92, 10, 11, 76, 116, 9, 69,
        44, 88, 36, 37, 124, 84, 40, 85, 13, 93, 77, 18, 62, 14, 128, 117, 98, 110, 45, 12, 70, 50, 89, 125,
        41, 94, 78, 79, 63, 99, 15, 56, 118, 111, 46, 71, 51, 129, 90, 142, 126, 42, 95, 104, 100, 64, 43, 57,
        91, 127, 119, 112, 47, 130, 52, 72, 73, 96, 143, 97, 105, 140, 101, 65, 58, 120, 113, 121, 48, 53, 49, 145,
        106, 146, 102, 131, 66, 147, 132, 59, 141, 148, 114, 149, 54, 150, 138, 107, 55, 103, 115, 67, 60, 61, 134, 133,
        108, 136, 109, 151, 152, 153, 154, 139, 155, 156, 135, 137, 144,
    ),
)
RECORD = None
COPIES = 120
DIRECT = ()
PIECE = 512
HALVES = ((0, 8, 7, 15, 1, 9, 2, 10), (6, 14, 3, 11, 5, 13, 4, 12))

gelu_const = math.sqrt(2.0 / math.pi)
bf16, f32 = jnp.bfloat16, jnp.float32


def gelu_and_slope(value):
    tangent = jnp.tanh(gelu_const * (value + 0.044715 * value * value * value))
    half = 0.5 * (1.0 + tangent)
    slope = half + 0.5 * value * (1.0 - tangent * tangent) * gelu_const * (
        1.0 + 3.0 * 0.044715 * value * value
    )
    return value * half, slope


def contract(left, right, dims):
    return lax.dot_general(left, right, ((dims[:1], dims[1:]), ((), ())), preferred_element_type=f32)


class at:
    def __init__(self, ref):
        self.ref, self.index = ref, ()

    def __getitem__(self, index):
        self.index = index
        return self

    def __call__(self):
        return self.ref.at[self.index]


class Names:
    def __init__(self):
        self.known = {}

    def __call__(self, name):
        return self.known.setdefault(name, len(self.known))


def kernel(
    x_hbm, g_hbm, wu_hbm, wd_hbm, dx_out, up_out, down_out,
    XG, WU, WD, PART, PART16, IN, S2, AD, AT, Q, PS, PR,
    XS, XR, ZS, ZR, ACC, local_sem, send_sem, recv_sem,
):
    width, units = WU.shape
    piece = ACC.shape[3]
    core, z, x, y = (lax.axis_index(a) for a in ("dp", "z", "x", "y"))
    partner = {"dp": 1 - core}
    left_z, right_z = {"z": (z + NZ - 1) % NZ}, {"z": (z + 1) % NZ}
    left_x, right_x = {"x": (x + NX - 1) % NX}, {"x": (x + 1) % NX}
    ya = y + 1 - 2 * (y % 2)
    yb = 3 - y
    yab = 3 - ya
    near_a, near_b = {"y": ya}, {"y": yb}
    away_y = {"y": yab}
    away_x = [{"x": (x + d) % NX} for d in range(NX)]
    away_z = [{"z": (z + d) % NZ} for d in range(NZ)]
    links = {id(partner): "p", id(left_z): "z-", id(right_z): "z+", id(left_x): "x-", id(right_x): "x+"}
    links.update({id(near_a): "a", id(near_b): "b", id(away_y): ("y", 2)})
    links.update({id(device): ("z", d) for d, device in enumerate(away_z)})
    links.update({id(device): ("x", d) for d, device in enumerate(away_x)})
    names = Names()

    def log(kind, *what):
        if RECORD is not None:
            RECORD.append((kind, *what))

    def send(src, dst, device, name, group):
        log("send", links[id(device)], name, math.prod(src().shape) * src().dtype.itemsize)
        pltpu.make_async_remote_copy(
            src_ref=src(),
            dst_ref=dst(),
            send_sem=send_sem.at[group],
            recv_sem=recv_sem.at[names(name)],
            device_id=device,
            device_id_type=MESH,
        ).start()

    def recv(dst, name):
        log("recv", name)
        pltpu.make_async_remote_copy(
            src_ref=dst(),
            dst_ref=dst(),
            send_sem=send_sem.at[0],
            recv_sem=recv_sem.at[names(name)],
            device_id=partner,
            device_id_type=MESH,
        ).wait_recv()

    def sent(src, group):
        pltpu.make_async_remote_copy(
            src_ref=src(),
            dst_ref=src(),
            send_sem=send_sem.at[group],
            recv_sem=recv_sem.at[0],
            device_id=partner,
            device_id_type=MESH,
        ).wait_send()

    barrier = pltpu.get_barrier_semaphore()
    near = (partner, left_z, right_z, left_x, right_x, away_x[2], near_a, near_b)
    for device in near:
        pl.semaphore_signal(barrier, inc=1, device_id=device, device_id_type=MESH)
    local = [
        pltpu.make_async_copy(src, dst, local_sem.at[k])
        for k, (src, dst) in enumerate(
            ((x_hbm, XG.at[0, 0, 0, 0]), (g_hbm, XG.at[0, 0, 0, 1]), (wu_hbm, WU), (wd_hbm, WD))
        )
    ]
    for copy in local:
        copy.start()
    pl.semaphore_wait(barrier, len(near))
    local[0].wait()
    local[1].wait()

    def hand(pz_from, pz_to, px_from, px_to, device, a=None):
        group = 1 if px_from != px_to else 8 if pz_to == 4 else 0
        if a is None:
            src, dst = at(XG)[0, pz_from, px_from], at(XG)[0, pz_to, px_to]
        else:
            src, dst = at(XG)[0, pz_from, px_from, a], at(XG)[0, pz_to, px_to, a]
        send(src, dst, device, ("xg", pz_to, px_to), group)

    def get(pz, px):
        recv(at(XG)[0, pz, px], ("xg", pz, px))

    def spread_z(px):
        hand(0, NZ - 1, px, px, right_z)
        hand(0, 1, px, px, left_z)

    def spread_x(pz):
        hand(pz, pz, 0, NX - 1, right_x)
        hand(pz, pz, 0, 1, left_x)
        if pz == 0:
            hand(pz, pz, 0, 2, away_x[2])

    def pair(pz, px):
        send(at(XG)[0, pz, px], at(XG)[1, pz, px], partner, ("pair", pz), 2)

    def begin():
        spread_x(0)
        spread_z(0)
        pair(0, 0)

    def step_x(pz, s, then):
        px = (3, 1)[s]
        get(pz, px)
        if pz:
            hand(pz, pz, px, 2, (right_x, left_x)[s], s)
        then(pz, px)
        pair(pz, px)

    def end_x(pz, then):
        get(pz, 2)
        then(pz, 2)
        pair(pz, 2)

    def step_z(d, px, s, then):
        pz = (NZ - d, d)[s]
        get(pz, px)
        beyond = pz - 1 if s == 0 else pz + 1
        if beyond != 4 or px == 0:
            hand(pz, beyond, px, px, (right_z, left_z)[s], s if beyond == 4 else None)
        then(pz, px)
        pair(pz, px)

    def end_z(px, then):
        get(4, px)
        then(4, px)
        pair(4, px)

    def nothing(pz, px):
        pass

    def along_z(pz, px):
        spread_z(px)

    def along_x(pz, px):
        spread_x(pz)

    def tokens(c, a, columns=slice(None)):
        return XG[c // NZ, c % NZ, :, a, :, columns].reshape(NX * 16, -1)

    def products(pz):
        if pz >= NZ:
            recv(at(XG)[1, pz - NZ], ("pair", pz - NZ))
        for a, (weights, dims) in enumerate(((WU, (1, 0)), (WD, (1, 1)))):
            part = contract(tokens(pz, a), weights[...], dims)
            part = part.reshape(4, NX * 4, units)
            PART[pz, a] = part
            PART16[pz, a] = part.astype(bf16)
        ways = ((near_a, ya), (near_b, yb), (away_y, yab))
        if pz in DIRECT:
            for k in (2, 0, 1):
                for a in range(2):
                    src = at(PART16)[pz, a, ways[k][1]]
                    send(src, at(IN)[pz, a, k], ways[k][0], ("in", pz), 4 if k == 2 else 3)
            return
        for a in range(2):
            send(at(PART16)[pz, a, yab], at(IN)[pz, a, 2], ways[a][0], ("half", pz), 3)
        for a in range(2):
            send(at(PART16)[pz, a, ways[a][1]], at(IN)[pz, a, 0], ways[a][0], ("in", pz), 3)

    def second(pz):
        recv(at(IN)[pz, :, 2], ("half", pz))
        for a, device, owner in ((0, near_b, yb), (1, near_a, ya)):
            S2[pz, a] = (PART[pz, a, owner] + IN[pz, a, 2].astype(f32)).astype(bf16)
            send(at(S2)[pz, a], at(IN)[pz, a, 1], device, ("in", pz), 4)

    def activate(pz):
        parts = 3 if pz in DIRECT else 2
        recv(at(IN)[pz, :, :parts], ("in", pz))
        sums = []
        for a in range(2):
            value = PART[pz, a, y]
            for k in range(parts):
                value = value + IN[pz, a, k].astype(f32)
            sums.append(value)
        active, slope = gelu_and_slope(sums[0])
        AD[pz, 0, y] = active.astype(bf16)
        AD[pz, 1, y] = (sums[1] * slope).astype(bf16)
        own = [at(AD)[pz, a, y] for a in range(2)]
        if pz in DIRECT:
            for a in (1, 0):
                send(own[a], own[a], away_y, ("rest", pz), 4)
        for a, device in ((0, near_b), (1, near_a)):
            send(own[a], own[a], device, ("first", pz), 4)
        for a, device in ((0, near_a), (1, near_b)):
            send(own[a], own[a], device, ("rest", pz), 4)

    def pass_on(pz):
        recv(at(S2)[pz], ("first", pz))
        if pz not in DIRECT:
            for a, owner, device in ((0, yb, near_a), (1, ya, near_b)):
                send(at(AD)[pz, a, owner], at(AD)[pz, a, owner], device, ("rest", pz), 4)

    def inward(pz):
        recv(at(AD)[pz, 0], ("rest", pz))
        delta = AD[pz, 1].reshape(NX * 16, units)
        back = contract(delta, WU[...], (1, 1)).reshape(NX, 16, width)
        if pz < NZ:
            Q[pz] = back
        else:
            PS[pz - NZ] = back
            send(at(PS)[pz - NZ], at(PR)[pz - NZ], partner, ("back", pz - NZ), 5)

    def turn(pz):
        place = (HALVES[0] + HALVES[1]).index(pz)
        rows = slice(place * NX * 16, (place + 1) * NX * 16)
        for a in range(2):
            AT[a, :, rows] = AD[pz, a].reshape(NX * 16, units).T

    def rows(pz):
        recv(at(PR)[pz], ("back", pz))
        for px in (2, 1, 3):
            XS[pz, px - 1] = (Q[pz, px] + PR[pz, px]).astype(bf16)
            send(at(XS)[pz, px - 1], at(XR)[pz, px - 1], away_x[px], ("x", pz), 6)

    def rows_last(pz):
        value = Q[pz, 0] + PR[pz, 0]
        recv(at(XR)[pz], ("x", pz))
        for px in (1, 3, 2):
            value = value + XR[pz, px - 1].astype(f32)
        if pz == 0:
            Q[0, 0] = value
        else:
            ZS[pz - 1] = value.astype(bf16)
            send(at(ZS)[pz - 1], at(ZR)[pz - 1], away_z[pz], ("z",), 7)

    def finish():
        value = Q[0, 0]
        recv(lambda: ZR, ("z",))
        for pz in range(1, NZ):
            value = value + ZR[pz - 1].astype(f32)
        dx_out[...] = value.astype(bf16)

    def weights(n, a, part):
        columns = slice(n * piece, (n + 1) * piece)
        group = HALVES[part]
        every = jnp.concatenate([tokens(pz, a, columns) for pz in group], axis=0)
        low = part * 8 * NX * 16
        grad = contract(AT[1 - a, :, low : low + 8 * NX * 16], every, (1, 0))
        if part == 0:
            ACC[a, n] = grad
        elif a == 0:
            up_out[columns, :] = ((ACC[a, n] + grad) * 0.5).T.astype(bf16)
        else:
            down_out[:, columns] = ((ACC[a, n] + grad) * 0.5).astype(bf16)

    def tasks(number):
        every = {("begin",): (begin, ())}
        for pz in (0, 4) if number == 0 else range(NZ):
            then = along_z if number == 0 and pz == 0 else nothing
            for s in range(2):
                every["x", pz, s] = (functools.partial(step_x, pz, s, then), ())
            every["end_x", pz] = (functools.partial(end_x, pz, then), ())
        for px in range(NX) if number == 0 else (0,):
            for d in (1, 2, 3):
                for s in range(2):
                    then = along_x if number == 1 else nothing
                    every["z", d, px, s] = (functools.partial(step_z, d, px, s, then), ())
        every["end_z", 0] = (functools.partial(end_z, 0, along_x), ())
        for c in range(2 * NZ):
            pz = c % NZ
            own = [k for k in every if k[0] in ("x", "end_x") and k[1] == pz]
            if pz == 4:
                own += [k for k in every if k[0] == "end_z"]
            elif pz:
                own += [k for k in every if k[0] == "z" and (NZ - k[1], k[1])[k[3]] == pz]
            every["products", c] = (functools.partial(products, c), tuple(own) if c < NZ else ())
            step = (lambda: None) if c in DIRECT else functools.partial(second, c)
            every["second", c] = (step, (("products", c),))
            every["activate", c] = (functools.partial(activate, c), (("products", c),))
            every["pass", c] = (functools.partial(pass_on, c), (("activate", c),))
            every["inward", c] = (functools.partial(inward, c), (("pass", c),))
            every["turn", c] = (functools.partial(turn, c), (("inward", c),))
        for pz in range(NZ):
            every["rows", pz] = (functools.partial(rows, pz), (("inward", pz),))
            every["rows3", pz] = (functools.partial(rows_last, pz), (("rows", pz),))
        every["finish",] = (finish, (("rows3", 0),))
        for part in range(2):
            turned = tuple(("turn", pz) for pz in HALVES[part])
            for a in range(2):
                for n in range(width // piece):
                    after = turned + ((("weights", n, a, 0),) if part else ())
                    every["weights", n, a, part] = (functools.partial(weights, n, a, part), after)
        return every

    def whole_core(number):
        @pl.when(core == number)
        def _():
            every = tasks(number)
            known = list(every)
            for step in ORDER[number] or range(len(known)):
                name = known[step]
                body, after = every.pop(name)
                log("task", number, name, after)
                if name[0] == "products" and not any(k[0] == "products" for k in done):
                    local[2].wait()
                    local[3].wait()
                done.append(name)
                scope(name, body)
            done.clear()
            if number == 0:
                sent(at(XG)[0, 1:7], 0)
                sent(at(XG)[0, 1:3, 1:4], 1)
            else:
                sent(at(XG)[0, 1:7, 0], 0)
                sent(at(XG)[0, :, 1:4], 1)
            sent(at(XG)[0, 4, 0], 8)
            for group, ref in ((2, XG.at[0]), (3, PART16.at[:, 0]), (4, PART16), (5, PS), (6, XS), (7, ZS)):
                sent(lambda ref=ref: ref, group)

    def scope(name, body):
        body()

    done = []
    whole_core(0)
    whole_core(1)
    assert len(names.known) <= COPIES


def put_out(*refs):
    copies = [pltpu.make_async_copy(refs[0], refs[3], refs[6].at[0])]
    for k in (1, 2):
        rows = refs[k].shape[0] // 4
        for n in range(4):
            part = pl.ds(n * rows, rows)
            src, dst = refs[k].at[part], refs[3 + k].at[part]
            copies.append(pltpu.make_async_copy(src, dst, refs[6].at[len(copies)]))
    for copy in copies:
        copy.start()
    for copy in copies:
        copy.wait()


def shards(inputs, up_weight, down_weight, cotangent):
    rows, width = inputs.shape
    units = up_weight.shape[1]
    seg = NX * rows // 4
    piece = min(PIECE, width)
    vmem = pltpu.VMEM
    anywhere = pl.BlockSpec(memory_space=pl.ANY)
    whole = pl.BlockSpec(memory_space=pltpu.VMEM)
    results = pl.pallas_call(
        kernel,
        out_shape=(
            pltpu.VMEM((rows, width), bf16),
            pltpu.VMEM((width, units), bf16),
            pltpu.VMEM((units, width), bf16),
        ),
        in_specs=[anywhere] * 4,
        out_specs=(whole, whole, whole),
        scratch_shapes=[
            vmem((2, NZ, NX, 2, rows, width), bf16),
            vmem((width, units), bf16),
            vmem((units, width), bf16),
            vmem((2 * NZ, 2, 4, seg, units), f32),
            vmem((2 * NZ, 2, 4, seg, units), bf16),
            vmem((2 * NZ, 2, 3, seg, units), bf16),
            vmem((2 * NZ, 2, seg, units), bf16),
            vmem((2 * NZ, 2, 4, seg, units), bf16),
            vmem((2, units, 8 * NZ * seg), bf16),
            vmem((NZ, NX, rows, width), f32),
            vmem((NZ, NX, rows, width), f32),
            vmem((NZ, NX, rows, width), f32),
            vmem((NZ, NX - 1, rows, width), bf16),
            vmem((NZ, NX - 1, rows, width), bf16),
            vmem((NZ - 1, rows, width), bf16),
            vmem((NZ - 1, rows, width), bf16),
            vmem((2, width // piece, units, piece), f32),
            pltpu.SemaphoreType.DMA((4,)),
            pltpu.SemaphoreType.DMA((9,)),
            pltpu.SemaphoreType.DMA((COPIES,)),
        ],
        compiler_params=pltpu.CompilerParams(
            collective_id=0, has_side_effects=True, vmem_limit_bytes=52 << 20
        ),
    )(inputs, cotangent, up_weight, down_weight)
    return pl.pallas_call(
        put_out,
        out_shape=tuple(jax.ShapeDtypeStruct(r.shape, r.dtype) for r in results),
        in_specs=[whole] * 3,
        out_specs=(anywhere,) * 3,
        scratch_shapes=[pltpu.SemaphoreType.DMA((9,))],
        compiler_params=pltpu.CompilerParams(vmem_limit_bytes=4 << 20),
    )(*results)


def solution(mesh):
    torus = Mesh(mesh.devices.reshape(2, NZ, NX, NY), ("dp", "z", "x", "y"))
    return jax.shard_map(
        shards,
        mesh=torus,
        in_specs=(P(DP_ROW, "y"), P("y", DP_ROW), P(DP_ROW, "y"), P(DP_ROW, "y")),
        out_specs=(P(DP_ROW, "y"), P("y", DP_ROW), P(DP_ROW, "y")),
        check_vma=False,
    )
```

```python
import functools
import math

import jax
import jax.numpy as jnp
from jax import lax
from jax.experimental import pallas as pl
from jax.experimental.pallas import tpu as pltpu
from jax.sharding import Mesh
from jax.sharding import PartitionSpec as P

NZ, NX, NY = 8, 4, 4
DP_ROW = ("dp", "z", "x")
MESH = pl.DeviceIdType.MESH

ORDER = (
    (
        0, 4, 2, 1, 5, 3, 6, 12, 11, 32, 26, 7, 25, 18, 19, 42, 33, 14, 34, 8, 13, 28, 102, 43,
        9, 27, 44, 35, 20, 21, 52, 16, 92, 15, 103, 45, 104, 36, 10, 30, 37, 29, 23, 53, 62, 22, 54, 94,
        17, 93, 47, 31, 46, 105, 24, 63, 82, 38, 40, 55, 64, 39, 72, 95, 48, 107, 49, 106, 83, 84, 57, 56,
        41, 50, 74, 65, 73, 97, 96, 108, 110, 109, 85, 58, 51, 66, 67, 59, 75, 98, 100, 99, 87, 113, 114, 86,
        111, 68, 60, 76, 77, 69, 115, 116, 117, 118, 101, 70, 88, 90, 89, 78, 80, 79, 119, 120, 121, 61, 122, 123,
        124, 71, 91, 81, 112,
    ),
    (
        0, 26, 2, 1, 25, 5, 4, 28, 3, 32, 27, 22, 23, 6, 8, 34, 7, 33, 30, 20, 42, 19, 24, 102,
        29, 35, 9, 43, 11, 10, 44, 21, 104, 103, 92, 36, 37, 17, 31, 52, 16, 45, 12, 105, 94, 93, 62, 14,
        53, 13, 54, 38, 18, 39, 82, 46, 47, 106, 107, 15, 72, 95, 63, 64, 55, 83, 84, 40, 48, 49, 50, 73,
        74, 108, 109, 96, 97, 41, 65, 57, 56, 85, 51, 75, 98, 99, 113, 66, 67, 110, 114, 86, 87, 115, 77, 58,
        60, 76, 59, 116, 117, 100, 118, 68, 111, 88, 70, 78, 79, 89, 69, 119, 61, 120, 121, 122, 90, 123, 101, 80,
        124, 71, 91, 81, 112,
    ),
)
RECORD = None
COPIES = 171
PIECE = 512
HALVES = ((0, 7, 1, 6), (2, 3, 5, 4))

gelu_const = math.sqrt(2.0 / math.pi)
bf16, f32 = jnp.bfloat16, jnp.float32


def gelu_and_slope(value):
    tangent = jnp.tanh(gelu_const * (value + 0.044715 * value * value * value))
    half = 0.5 * (1.0 + tangent)
    slope = half + 0.5 * value * (1.0 - tangent * tangent) * gelu_const * (
        1.0 + 3.0 * 0.044715 * value * value
    )
    return value * half, slope


def contract(left, right, dims):
    return lax.dot_general(left, right, ((dims[:1], dims[1:]), ((), ())), preferred_element_type=f32)


class at:
    def __init__(self, ref):
        self.ref, self.index = ref, ()

    def __getitem__(self, index):
        self.index = index
        return self

    def __call__(self):
        return self.ref.at[self.index]


class Names:
    def __init__(self):
        self.known = {}

    def __call__(self, name):
        return self.known.setdefault(name, len(self.known))


def kernel(
    x_hbm, g_hbm, wu_hbm, wd_hbm, dx_out, up_out, down_out,
    XG, WU, WD, PART, PART16, R1, S2, R2, AD, AT, Q, PS, PR,
    XS, XR, ZS, ZR, ACC, local_sem, send_sem, recv_sem,
):
    width, units = WU.shape
    piece = ACC.shape[3]
    core, z, x, y = (lax.axis_index(a) for a in ("dp", "z", "x", "y"))
    partner = {"dp": 1 - core}
    left_z, right_z = {"z": (z + NZ - 1) % NZ}, {"z": (z + 1) % NZ}
    left_x, right_x = {"x": (x + NX - 1) % NX}, {"x": (x + 1) % NX}
    ya = y + 1 - 2 * (y % 2)
    yb = 3 - y
    yab = 3 - ya
    near_a, near_b = {"y": ya}, {"y": yb}
    away_x = [{"x": (x + d) % NX} for d in range(NX)]
    away_z = [{"z": (z + d) % NZ} for d in range(NZ)]
    links = {id(partner): "p", id(left_z): "z-", id(right_z): "z+", id(left_x): "x-", id(right_x): "x+"}
    links.update({id(near_a): "a", id(near_b): "b"})
    links.update({id(device): ("z", d) for d, device in enumerate(away_z)})
    links.update({id(device): ("x", d) for d, device in enumerate(away_x)})
    names = Names()

    def log(kind, *what):
        if RECORD is not None:
            RECORD.append((kind, *what))

    def send(src, dst, device, name, group):
        log("send", links[id(device)], name, math.prod(src().shape) * src().dtype.itemsize)
        pltpu.make_async_remote_copy(
            src_ref=src(),
            dst_ref=dst(),
            send_sem=send_sem.at[group],
            recv_sem=recv_sem.at[names(name)],
            device_id=device,
            device_id_type=MESH,
        ).start()

    def recv(dst, name):
        log("recv", name)
        pltpu.make_async_remote_copy(
            src_ref=dst(),
            dst_ref=dst(),
            send_sem=send_sem.at[0],
            recv_sem=recv_sem.at[names(name)],
            device_id=partner,
            device_id_type=MESH,
        ).wait_recv()

    def sent(src, group):
        pltpu.make_async_remote_copy(
            src_ref=src(),
            dst_ref=src(),
            send_sem=send_sem.at[group],
            recv_sem=recv_sem.at[0],
            device_id=partner,
            device_id_type=MESH,
        ).wait_send()

    barrier = pltpu.get_barrier_semaphore()
    near = (partner, left_z, right_z, left_x, right_x, near_a, near_b)
    for device in near:
        pl.semaphore_signal(barrier, inc=1, device_id=device, device_id_type=MESH)
    local = [
        pltpu.make_async_copy(src, dst, local_sem.at[k])
        for k, (src, dst) in enumerate(
            ((x_hbm, XG.at[0, 0, 0, 0]), (g_hbm, XG.at[0, 0, 0, 1]), (wu_hbm, WU), (wd_hbm, WD))
        )
    ]
    for copy in local:
        copy.start()
    pl.semaphore_wait(barrier, len(near))
    local[0].wait()
    local[1].wait()

    def hand(pz_from, pz_to, px_from, px_to, device, a=None):
        group = 0 if px_from == px_to else 1
        if a is None:
            src, dst = at(XG)[0, pz_from, px_from], at(XG)[0, pz_to, px_to]
        else:
            src, dst = at(XG)[0, pz_from, px_from, a], at(XG)[0, pz_to, px_to, a]
        send(src, dst, device, ("xg", pz_to, px_to, a), group)

    def get(pz, px, a=None):
        recv(at(XG)[0, pz, px] if a is None else at(XG)[0, pz, px, a], ("xg", pz, px, a))

    def spread_z(px):
        hand(0, NZ - 1, px, px, right_z)
        hand(0, 1, px, px, left_z)

    def spread_x(pz):
        hand(pz, pz, 0, NX - 1, right_x)
        hand(pz, pz, 0, 1, left_x)

    def pair(pz, px):
        send(at(XG)[0, pz, px], at(XG)[1, pz, px], partner, ("pair", pz), 2)

    def begin():
        spread_x(0)
        spread_z(0)
        pair(0, 0)

    def step_x(pz, s, then):
        px = (3, 1)[s]
        get(pz, px)
        hand(pz, pz, px, 2, (right_x, left_x)[s], s)
        then(pz, px)
        pair(pz, px)

    def end_x(pz, then):
        get(pz, 2, 0)
        get(pz, 2, 1)
        then(pz, 2)
        pair(pz, 2)

    def step_z(d, px, s, then):
        pz = (NZ - d, d)[s]
        get(pz, px)
        beyond = pz - 1 if s == 0 else pz + 1
        hand(pz, beyond, px, px, (right_z, left_z)[s], s if beyond == 4 else None)
        then(pz, px)
        pair(pz, px)

    def end_z(px, then):
        get(4, px, 0)
        get(4, px, 1)
        then(4, px)
        pair(4, px)

    def nothing(pz, px):
        pass

    def along_z(pz, px):
        spread_z(px)

    def along_x(pz, px):
        spread_x(pz)

    def tokens(pz, a, columns=slice(None)):
        return [XG[k, pz, :, a, :, columns].reshape(NX * 16, -1) for k in range(2)]

    def products(pz):
        recv(at(XG)[1, pz], ("pair", pz))
        for a, (weights, dims) in enumerate(((WU, (1, 0)), (WD, (1, 1)))):
            part = contract(jnp.concatenate(tokens(pz, a), axis=0), weights[...], dims)
            part = part.reshape(4, NX * 8, units)
            PART[pz, a] = part
            PART16[pz, a] = part.astype(bf16)
        for k in (1, 0):
            for a, device, first in ((0, near_a, ya), (1, near_b, yb)):
                owner = yab if k else first
                send(at(PART16)[pz, a, owner], at(R1)[pz, a, k], device, ("r1", pz, a, k), 3)

    def second(pz, a):
        device, owner = ((near_b, yb), (near_a, ya))[a]
        recv(at(R1)[pz, a, 1], ("r1", pz, a, 1))
        S2[pz, a] = (PART[pz, a, owner] + R1[pz, a, 1].astype(f32)).astype(bf16)
        send(at(S2)[pz, a], at(R2)[pz, a], device, ("r2", pz, a), 4)

    def activate(pz):
        sums = []
        for a in range(2):
            recv(at(R1)[pz, a, 0], ("r1", pz, a, 0))
            recv(at(R2)[pz, a], ("r2", pz, a))
            sums.append(PART[pz, a, y] + R1[pz, a, 0].astype(f32) + R2[pz, a].astype(f32))
        active, slope = gelu_and_slope(sums[0])
        AD[pz, 0, y] = active.astype(bf16)
        AD[pz, 1, y] = (sums[1] * slope).astype(bf16)
        for a, device, side in ((0, near_b, "b"), (1, near_a, "a"), (0, near_a, "a"), (1, near_b, "b")):
            send(at(AD)[pz, a, y], at(AD)[pz, a, y], device, ("ad", pz, a, side), 4)

    def pass_on(pz, a):
        owner, device = ((yb, near_a), (ya, near_b))[a]
        recv(at(AD)[pz, a, owner], ("ad", pz, a, "ba"[a]))
        send(at(AD)[pz, a, owner], at(AD)[pz, a, owner], device, ("ad", pz, a, "ab"), 4)

    def inward(pz):
        for a, owner in ((1, yb), (0, ya)):
            recv(at(AD)[pz, a, owner], ("ad", pz, a, "ab"[a]))
            recv(at(AD)[pz, a, yab], ("ad", pz, a, "ab"))
        delta = AD[pz, 1].reshape(8 * NX * 4, units)
        back = contract(delta, WU[...], (1, 1)).reshape(2, NX, 16, width)
        PS[pz] = back[1].astype(bf16)
        send(at(PS)[pz], at(PR)[pz], partner, ("back", pz), 5)
        Q[pz] = back[0]

    def turn(pz):
        place = (HALVES[0] + HALVES[1]).index(pz)
        rows = slice(place * 8 * 16, (place + 1) * 8 * 16)
        for a in range(2):
            AT[a, :, rows] = AD[pz, a].reshape(8 * 16, units).T

    def rows(pz):
        recv(at(PR)[pz], ("back", pz))
        for px in (2, 1, 3):
            XS[pz, px - 1] = (Q[pz, px] + PR[pz, px].astype(f32)).astype(bf16)
            send(at(XS)[pz, px - 1], at(XR)[pz, px - 1], away_x[px], ("x", pz), 6)

    def rows_last(pz):
        value = Q[pz, 0] + PR[pz, 0].astype(f32)
        recv(at(XR)[pz], ("x", pz))
        for px in (1, 3, 2):
            value = value + XR[pz, px - 1].astype(f32)
        if pz == 0:
            Q[0, 0] = value
        else:
            ZS[pz - 1] = value.astype(bf16)
            send(at(ZS)[pz - 1], at(ZR)[pz - 1], away_z[pz], ("z",), 7)

    def finish():
        value = Q[0, 0]
        recv(lambda: ZR, ("z",))
        for pz in range(1, NZ):
            value = value + ZR[pz - 1].astype(f32)
        dx_out[...] = value.astype(bf16)

    def weights(n, a, part):
        columns = slice(n * piece, (n + 1) * piece)
        group = HALVES[part]
        every = jnp.concatenate([t for pz in group for t in tokens(pz, a, columns)], axis=0)
        low = part * 4 * 8 * 16
        grad = contract(AT[1 - a, :, low : low + 4 * 8 * 16], every, (1, 0))
        if part == 0:
            ACC[a, n] = grad
        elif a == 0:
            up_out[columns, :] = ((ACC[a, n] + grad) * 0.5).T.astype(bf16)
        else:
            down_out[:, columns] = ((ACC[a, n] + grad) * 0.5).astype(bf16)

    def tasks(number):
        every = {("begin",): (begin, ())}
        far, near_then, far_then = (
            ((0,), along_z, nothing) if number == 0 else (range(NZ), nothing, along_x)
        )
        for pz in far:
            for s in range(2):
                every["x", pz, s] = (functools.partial(step_x, pz, s, near_then), ())
            every["end_x", pz] = (functools.partial(end_x, pz, near_then), ())
        for px in range(NX) if number == 0 else (0,):
            for d in (1, 2, 3):
                for s in range(2):
                    every["z", d, px, s] = (functools.partial(step_z, d, px, s, far_then), ())
            every["end_z", px] = (functools.partial(end_z, px, far_then), ())
        for pz in range(NZ):
            own = [k for k in every if k[0] in ("x", "end_x") and k[1] == pz]
            if pz == 4:
                own += [k for k in every if k[0] == "end_z"]
            elif pz:
                own += [k for k in every if k[0] == "z" and (NZ - k[1], k[1])[k[3]] == pz]
            every["products", pz] = (functools.partial(products, pz), tuple(own))
            for a in range(2):
                every["second", pz, a] = (functools.partial(second, pz, a), (("products", pz),))
            every["activate", pz] = (functools.partial(activate, pz), (("products", pz),))
            for a in range(2):
                every["pass", pz, a] = (functools.partial(pass_on, pz, a), (("activate", pz),))
            passed = (("pass", pz, 0), ("pass", pz, 1))
            every["inward", pz] = (functools.partial(inward, pz), passed)
            every["turn", pz] = (functools.partial(turn, pz), (("inward", pz),))
            every["rows", pz] = (functools.partial(rows, pz), (("inward", pz),))
            every["rows3", pz] = (functools.partial(rows_last, pz), (("rows", pz),))
        every["finish",] = (finish, (("rows3", 0),))
        for part in range(2):
            turned = tuple(("turn", pz) for pz in HALVES[part])
            for a in range(2):
                for n in range(width // piece):
                    after = turned + ((("weights", n, a, 0),) if part else ())
                    every["weights", n, a, part] = (functools.partial(weights, n, a, part), after)
        return every

    def whole_core(number):
        @pl.when(core == number)
        def _():
            every = tasks(number)
            known = list(every)
            for step in ORDER[number] or range(len(known)):
                name = known[step]
                body, after = every.pop(name)
                log("task", number, name, after)
                if name[0] == "products" and not any(k[0] == "products" for k in done):
                    local[2].wait()
                    local[3].wait()
                done.append(name)
                scope(name, body)
            done.clear()
            if number == 0:
                sent(at(XG)[0, 1:8], 0)
                sent(at(XG)[0, 0, 1:4], 1)
            else:
                sent(at(XG)[0, 1:8, 0], 0)
                sent(at(XG)[0, :, 1:4], 1)
            for group, ref in ((2, XG.at[0]), (3, R1), (4, PART16), (5, PS), (6, XS), (7, ZS)):
                sent(lambda ref=ref: ref, group)

    def scope(name, body):
        body()

    done = []
    whole_core(0)
    whole_core(1)
    assert len(names.known) <= COPIES


def put_out(*refs):
    copies = [pltpu.make_async_copy(refs[k], refs[3 + k], refs[6].at[k]) for k in range(3)]
    for copy in copies:
        copy.start()
    for copy in copies:
        copy.wait()


def shards(inputs, up_weight, down_weight, cotangent):
    rows, width = inputs.shape
    units = up_weight.shape[1]
    seg = NX * rows // 2
    piece = min(PIECE, width)
    vmem = pltpu.VMEM
    anywhere = pl.BlockSpec(memory_space=pl.ANY)
    whole = pl.BlockSpec(memory_space=pltpu.VMEM)
    results = pl.pallas_call(
        kernel,
        out_shape=(
            pltpu.VMEM((rows, width), bf16),
            pltpu.VMEM((width, units), bf16),
            pltpu.VMEM((units, width), bf16),
        ),
        in_specs=[anywhere] * 4,
        out_specs=(whole, whole, whole),
        scratch_shapes=[
            vmem((2, NZ, NX, 2, rows, width), bf16),
            vmem((width, units), bf16),
            vmem((units, width), bf16),
            vmem((NZ, 2, 4, seg, units), f32),
            vmem((NZ, 2, 4, seg, units), bf16),
            vmem((NZ, 2, 2, seg, units), bf16),
            vmem((NZ, 2, seg, units), bf16),
            vmem((NZ, 2, seg, units), bf16),
            vmem((NZ, 2, 4, seg, units), bf16),
            vmem((2, units, NZ * 4 * seg), bf16),
            vmem((NZ, NX, rows, width), f32),
            vmem((NZ, NX, rows, width), bf16),
            vmem((NZ, NX, rows, width), bf16),
            vmem((NZ, NX - 1, rows, width), bf16),
            vmem((NZ, NX - 1, rows, width), bf16),
            vmem((NZ - 1, rows, width), bf16),
            vmem((NZ - 1, rows, width), bf16),
            vmem((2, width // piece, units, piece), f32),
            pltpu.SemaphoreType.DMA((4,)),
            pltpu.SemaphoreType.DMA((8,)),
            pltpu.SemaphoreType.DMA((COPIES,)),
        ],
        compiler_params=pltpu.CompilerParams(
            collective_id=0, has_side_effects=True, vmem_limit_bytes=52 << 20
        ),
    )(inputs, cotangent, up_weight, down_weight)
    return pl.pallas_call(
        put_out,
        out_shape=tuple(jax.ShapeDtypeStruct(r.shape, r.dtype) for r in results),
        in_specs=[whole] * 3,
        out_specs=(anywhere,) * 3,
        scratch_shapes=[pltpu.SemaphoreType.DMA((3,))],
        compiler_params=pltpu.CompilerParams(vmem_limit_bytes=4 << 20),
    )(*results)


def solution(mesh):
    torus = Mesh(mesh.devices.reshape(2, NZ, NX, NY), ("dp", "z", "x", "y"))
    return jax.shard_map(
        shards,
        mesh=torus,
        in_specs=(P(DP_ROW, "y"), P("y", DP_ROW), P(DP_ROW, "y"), P(DP_ROW, "y")),
        out_specs=(P(DP_ROW, "y"), P("y", DP_ROW), P(DP_ROW, "y")),
        check_vma=False,
    )
```
